256 devices in a mesh: req: 32 (over y, x, z_hi), tp: 8 (over z_lo, core).
Axes of the slice: x: 4, y: 4, z: 8 (z_hi: 2, z_lo: 4; z = z_hi * 4 + z_lo), core: 2. Of those that a mesh axis runs over, the one named last changes fastest.
Arguments:
- residual: bfloat16 [8192, 2304], P('req'), may hold values from -58 to 58
- context: bfloat16 [8192, 2304], P('req', 'tp'), may hold values from -6 to 6
- attention_output_weight: bfloat16 [2304, 2304], P('tp'), may hold values from -0.1875 to 0.1875
- adapter_down_maps: bfloat16 [64, 2304, 16], P('req', 'tp'), may hold values from -0.125 to 0.125
- adapter_up_maps: bfloat16 [64, 16, 2304], P('req'), may hold values from -1.5 to 1.5
- adapter_storage_row: int32 [64], replicated, may hold values from 0 to 63, each once
- active_adapters: int32 [16], replicated, may hold values from 0 to 63, as said below
- request_token_length: int32 [32, 4], P('req'), may hold values from 1 to 128, 256 in all within a row
- request_adapter_entry: int32 [32, 4], P('req'), may hold values from 0 to 15
- expert_norm_gain: bfloat16 [2304], replicated, may hold values from 0.099609375 to 1.8984375
- router_projection: bfloat16 [2304, 8], replicated, may hold values from -0.125 to 0.125
- expert_choice_pairs: int32 [8192, 2], P('req'), may hold values from 0 to 7, all different within a row; in each aligned block of 256 rows (0 to 255, 256 to 511, ...) at most 80 rows name the same one
- expert_gate_weight: bfloat16 [32, 2304, 5760], P('req', None, 'tp'), as said below
- expert_up_weight: bfloat16 [32, 2304, 5760], P('req', None, 'tp'), as said below
- expert_down_weight: bfloat16 [32, 5760, 2304], P('req', 'tp'), as said below
Outputs:
- layer_out: bfloat16 [8192, 2304], P('req', 'tp')
The draws below stay inside these ranges and needn't reach their ends.
Inputs may be any that keep to these rules, and one draw needn't show every extreme that they name: `active_adapters`: 16 different adapter numbers, 0 and 63 among them. `adapter_storage_row`: every stored row appears once. `request_token_length`: each group's lengths sum to 256; the longest request of a group has exactly half of 256 tokens. `expert_choice_pairs`: each row names two different experts; within the 256 rows of one group no expert is named by more than 80 rows, a bound that some block reaches. `expert_gate_weight`: the 4 holders c * 8 + e of expert e hold the same weights. `expert_up_weight`: the 4 holders c * 8 + e of expert e hold the same weights. `expert_down_weight`: the 4 holders c * 8 + e of expert e hold the same weights.
All inputs are finite; a program needn't handle non-finite values.
Results may differ from the reference program's by a relative error of at most 0.0095.
Values may be sent and summed in bfloat16 or wider, within the bound.
A program may use at most 128 MiB of HBM per device.

```python
import math
import jax
import jax.numpy as jnp
import numpy as np
from jax import lax

MODEL_WIDTH = 2304
HEAD_COUNT = 36
HEAD_WIDTH = 64
EXPERTS = 8
FF = 5760
TOPK = 2
ADAPTER_RANK = 16
USED = 16
SLOTS = 4
GROUP_TOKENS = 256
CAP = 80
COPIES = 4
QUOTA = 20
BLOCKS = 32
TOKENS = 8192
ADAPTER_TOTAL = 64
N_TP = 8


def draw_residual(key, part):
    key_base, key_col, key_row = jax.random.split(key, 3)
    column = jnp.arange(MODEL_WIDTH, dtype=jnp.float32) / float(max(MODEL_WIDTH - 1, 1))
    col_scale = 10.0 ** (column - 0.5) * jnp.exp(jax.random.uniform(key_col, (MODEL_WIDTH,), minval=-0.5, maxval=0.5))
    row_scale = 10.0 ** (jax.random.uniform(key_row, (TOKENS, 1)) - 0.5)
    values = jnp.clip(jax.random.normal(key_base, (TOKENS, MODEL_WIDTH)), -3.5, 3.5)
    return (values * col_scale[None, :] * row_scale).astype(jnp.bfloat16)


def draw_active_adapters(key, part):
    middle_ids = jax.random.permutation(key, ADAPTER_TOTAL - 2)[:USED - 2].astype(jnp.int32) + 1
    edge_ids = jnp.array([0, ADAPTER_TOTAL - 1], dtype=jnp.int32)
    joined = jnp.concatenate([edge_ids, middle_ids])
    shuffle = jax.random.permutation(jax.random.fold_in(key, 11), USED)
    return joined[shuffle]


def held_weights(key, salt, rows_in, cols_out, fan_in):
    values = jnp.clip(jax.random.normal(jax.random.fold_in(key, salt), (EXPERTS, rows_in, cols_out)), -6.0, 6.0)
    scaled = values * float(fan_in) ** (-0.5)
    return jnp.tile(scaled, (COPIES, 1, 1)).astype(jnp.bfloat16)


def draw_expert_gate_weight(key, part):
    return held_weights(key, 21, MODEL_WIDTH, FF, MODEL_WIDTH)


def draw_expert_up_weight(key, part):
    return held_weights(key, 22, MODEL_WIDTH, FF, MODEL_WIDTH)


def draw_expert_down_weight(key, part):
    return held_weights(key, 23, FF, MODEL_WIDTH, FF)


def touch_ends(values, own_key, smallest, largest):
    spot = [jax.random.randint(jax.random.fold_in(own_key, axis), (), 0, length) for axis, length in enumerate(values.shape)]
    longest = values.shape.index(max(values.shape))
    neighbour = spot[:longest] + [(spot[longest] + 1) % values.shape[longest]] + spot[longest + 1:]
    return values.at[tuple(spot)].set(smallest).at[tuple(neighbour)].set(largest)


def with_spikes(values, stream_key, source, target, blocks, factor):
    def block_of(dim):
        return (jnp.arange(values.shape[dim]) // (values.shape[dim] // blocks)).reshape((-1,) + (1,) * (values.ndim - 1 - dim))

    one_side = jax.random.permutation(stream_key, blocks)[block_of(target)]
    other_side = (block_of(target) + blocks // 2) % blocks
    return jnp.where((block_of(source) == one_side) | (block_of(source) == other_side), factor * values, values)


def shard_levels(rng, shape, pieces, least, high):
    def one(axis_at, shards_of):
        heights = jax.random.uniform(jax.random.fold_in(jax.random.fold_in(rng, 6), axis_at), (shards_of,), jnp.float32, least / len(pieces), high / len(pieces))
        return jnp.repeat(jnp.exp(heights), shape[axis_at] // shards_of).reshape((-1,) + (1,) * (len(shape) - axis_at - 1))

    gain = one(*pieces[0])
    for cut in pieces[1:]:
        gain = gain * one(*cut)
    return gain


def rank_table(count, slope):
    loads = [(1 << 20) // math.isqrt(grade ** slope) + 1 for grade in range(1, count + 1)]
    scale = 1 + sum(loads) // (1 << 30)
    return np.cumsum(np.array([max(1, weight // scale) for weight in loads]))


def ranked_ids(own_key, extent, count, slope):
    listing = rank_table(count, slope)
    lot = jax.random.randint(jax.random.fold_in(own_key, 1), extent, 0, int(listing[count - 1]))
    rank = jnp.searchsorted(jnp.asarray(listing, jnp.int32), lot, side="right")
    return jax.random.permutation(jax.random.fold_in(own_key, 2), count)[rank].astype(jnp.int32)


def profile(count, total, bound, lean):
    weights = [(1 << 20) // math.isqrt(standing ** lean) + 1 for standing in range(2, count + 1)]
    surplus, holding = total - bound - (count - 1), [1] * (count - 1)
    while surplus > 0:
        free = [i for i in range(count - 1) if holding[i] < bound]
        mass, budget = sum([weights[i] for i in free]), surplus
        for i in free:
            addition = min(bound - holding[i], max(1, budget * weights[i] // mass), surplus)
            holding[i] = holding[i] + addition
            surplus = surplus - addition
    return np.array([bound] + holding)


def ragged(key, number_of, total, reach, slope):
    if number_of == 2:
        one = jax.random.randint(key, (), max(1, total - reach), min(reach, total - 1) + 1)
        return jnp.stack([one, total - one])
    lengths = jnp.asarray(profile(number_of, total, reach, slope), jnp.int32)
    couples = (number_of - 1) // 2
    giver, receiver = lengths[1:1 + 2 * couples:2], lengths[2:2 + 2 * couples:2]
    margin = jnp.minimum(giver - 1, reach - receiver)
    passed = jax.random.randint(jax.random.fold_in(key, 1), (couples,), 0, 1 << 20) % (margin + 1)
    lengths = lengths.at[1:1 + 2 * couples:2].set(giver - passed).at[2:2 + 2 * couples:2].set(receiver + passed)
    return lengths[jax.random.permutation(jax.random.fold_in(key, 2), number_of)]


def deal_out(key, own, number, rows, amount, top, limit, skew):
    ranking = jax.random.permutation(key, amount)
    heavy_load, usual = shares(amount, rows * top, limit, skew, True), shares(amount, rows * top, limit, skew, False)
    places = jnp.arange(amount)

    def named(tallies, offset_by):
        used = int((tallies > 0).sum())
        fixed = max(1, used // 4)
        passed = fixed + (places - fixed + offset_by * (used - fixed)) % max(1, amount - fixed)
        return jnp.zeros((amount,), jnp.int32).at[ranking[jnp.where(places < fixed, places, passed)]].set(jnp.asarray(tallies, jnp.int32))

    tallies = jnp.where(number % 4 == 0, named(heavy_load, number // 4), named(usual, number - number // 4 - 1))
    mixed = jax.random.permutation(jax.random.fold_in(own, 3), amount)
    source_of, sink = mixed[0:amount // 2 * 2:2], mixed[1:amount // 2 * 2:2]
    room = jnp.minimum(tallies[source_of] - 1, limit - tallies[sink]) // 2
    room = jnp.where((source_of == ranking[0]) | (sink == ranking[0]) | (tallies[sink] == 0), 0, jnp.maximum(room, 0))
    passed = jax.random.randint(jax.random.fold_in(own, 4), (amount // 2,), 0, 1 << 20) % (room + 1)
    tallies = tallies.at[source_of].add(-passed).at[sink].add(passed)
    items = jnp.searchsorted(jnp.cumsum(tallies), jnp.arange(rows * top), side="right").astype(jnp.int32)
    grid = items.reshape(top, rows).T
    grid = grid[jax.random.permutation(jax.random.fold_in(own, 1), rows)]
    offset_by = jax.random.randint(jax.random.fold_in(own, 2), (rows, 1), 0, top)
    return jnp.take_along_axis(grid, (jnp.arange(top)[None, :] + offset_by) % top, axis=1)


def shares(amount, total, most, lean, full):
    loads = [(1 << 20) // math.isqrt(standing ** lean) + 1 for standing in range(1, amount + 1)]
    largest = most if full else min(most, max(-(-total // amount), total * loads[0] // sum(loads)))
    least = 1 if total - largest >= amount - 1 else 0
    holding, rest = [largest] + [least] * (amount - 1), total - largest - least * (amount - 1)
    while rest > 0:
        movable = [i for i in range(1, amount) if holding[i] < largest] or [i for i in range(1, amount) if holding[i] < most]
        pool, left = sum([loads[i] for i in movable]), rest
        for i in movable:
            addition = min(most - holding[i], max(1, left * loads[i] // pool), rest)
            holding[i] = holding[i] + addition
            rest = rest - addition
    return np.array(holding)


def centred(key, extent, deviation, most, shards=(), kind=jnp.bfloat16):
    drawn = deviation * jax.random.normal(key, extent, jnp.float32)
    if shards:
        drawn = drawn * shard_levels(key, extent, shards, -0.22, 0.18)
    return jnp.clip(drawn, -most, most).astype(kind)


def heavy_noise(rng, extent, spread, most, cuts, heavy, kind=jnp.bfloat16):
    entries = spread * jax.random.normal(rng, extent, jnp.float32)
    if cuts:
        entries = entries * shard_levels(rng, extent, cuts, -0.22, 0.18)
    return jnp.clip(with_spikes(entries, jax.random.fold_in(rng, 3), *heavy), -most, most).astype(kind)


def setup_inputs(seed: int = 0) -> dict:
    seeds = jax.random.split(jax.random.key(seed), 16)
    residual = draw_residual(jax.random.fold_in(seeds[15], 71), 0)
    context = centred(seeds[1], (TOKENS, HEAD_COUNT * HEAD_WIDTH), 1.0, 6.0, ((0, 32), (1, 8)))
    attention_output_weight = heavy_noise(seeds[2], (HEAD_COUNT * HEAD_WIDTH, MODEL_WIDTH), (HEAD_COUNT * HEAD_WIDTH) ** -0.5, 0.1875, ((0, 8),), (0, 1, 8, 2.0))
    adapter_down_maps = centred(seeds[3], (ADAPTER_TOTAL, HEAD_COUNT * HEAD_WIDTH, ADAPTER_RANK), (HEAD_COUNT * HEAD_WIDTH) ** -0.5, 0.125, ((0, 32), (1, 8)))
    adapter_up_maps = centred(seeds[4], (ADAPTER_TOTAL, ADAPTER_RANK, MODEL_WIDTH), ADAPTER_RANK ** -0.5, 1.5, ((0, 32),))
    adapter_storage_row = jax.random.permutation(seeds[5], ADAPTER_TOTAL).astype(jnp.int32)
    active_adapters = draw_active_adapters(jax.random.fold_in(seeds[15], 71), 0)
    request_token_length = jax.vmap(lambda own: ragged(own, SLOTS, GROUP_TOKENS, GROUP_TOKENS // 2, 2))(jax.random.split(seeds[7], BLOCKS)).reshape((BLOCKS, SLOTS)).astype(jnp.int32)
    request_adapter_entry = touch_ends(ranked_ids(seeds[8], (BLOCKS, SLOTS), USED, 2), jax.random.fold_in(seeds[8], 3), 0, USED - 1).astype(jnp.int32)
    expert_norm_gain = jnp.clip(1.0 + 0.18 * jax.random.normal(seeds[9], (MODEL_WIDTH,), jnp.float32), 0.099609375, 1.8984375).astype(jnp.bfloat16)
    router_projection = centred(seeds[10], (MODEL_WIDTH, EXPERTS), MODEL_WIDTH ** -0.5, 0.125)
    expert_choice_pairs_keys = jax.random.split(jax.random.fold_in(seeds[11], 1), TOKENS // GROUP_TOKENS)
    expert_choice_pairs_turns = jax.random.permutation(jax.random.fold_in(seeds[11], 3), TOKENS // GROUP_TOKENS)
    expert_choice_pairs = jax.vmap(lambda own, number: deal_out(jax.random.fold_in(seeds[11], 2), own, number, GROUP_TOKENS, EXPERTS, TOPK, CAP, 2))(expert_choice_pairs_keys, expert_choice_pairs_turns).reshape((TOKENS, TOPK))
    expert_gate_weight = draw_expert_gate_weight(jax.random.fold_in(seeds[15], 71), 0)
    expert_up_weight = draw_expert_up_weight(jax.random.fold_in(seeds[15], 71), 0)
    expert_down_weight = draw_expert_down_weight(jax.random.fold_in(seeds[15], 71), 0)
    return {"residual": residual, "context": context, "attention_output_weight": attention_output_weight, "adapter_down_maps": adapter_down_maps, "adapter_up_maps": adapter_up_maps, "adapter_storage_row": adapter_storage_row, "active_adapters": active_adapters, "request_token_length": request_token_length, "request_adapter_entry": request_adapter_entry, "expert_norm_gain": expert_norm_gain, "router_projection": router_projection, "expert_choice_pairs": expert_choice_pairs, "expert_gate_weight": expert_gate_weight, "expert_up_weight": expert_up_weight, "expert_down_weight": expert_down_weight}


NORM_EPS = 1e-05

def token_picks(request_token_length, request_adapter_entry):
    bounds = jnp.cumsum(request_token_length, axis=1)
    position = jnp.arange(GROUP_TOKENS, dtype=jnp.int32)
    segment = lax.optimization_barrier(jnp.sum((position[None, :, None] >= bounds[:, None, :]).astype(jnp.int32), axis=2))
    return jnp.take_along_axis(request_adapter_entry, segment.astype(jnp.int32), axis=1)

def head_feature_total(context, attention_output_weight, adapter_down_maps, adapter_up_maps, adapter_stored_row):
    group_token_width = HEAD_COUNT * HEAD_WIDTH // N_TP
    out_groups = attention_output_weight.astype(jnp.float32).reshape(N_TP, group_token_width, MODEL_WIDTH)

    def one_block(block_args):
        ctx_block, row_block_span = block_args
        ctx_groups = ctx_block.astype(jnp.float32).reshape(GROUP_TOKENS, N_TP, group_token_width)
        token_down = adapter_down_maps[row_block_span].astype(jnp.float32).reshape(GROUP_TOKENS, N_TP, group_token_width, ADAPTER_RANK)
        token_up = adapter_up_maps[row_block_span].astype(jnp.float32)
        low_rank = jnp.einsum('tgf,tgfr->tgr', ctx_groups, token_down)
        low_rank = lax.optimization_barrier(low_rank.astype(jnp.bfloat16)).astype(jnp.float32)
        base_term = jnp.einsum('tgf,gfd->tgd', ctx_groups, out_groups)
        extra_term = jnp.einsum('tgr,trd->tgd', low_rank, token_up)
        rounded_parts = lax.optimization_barrier((base_term + extra_term).astype(jnp.bfloat16)).astype(jnp.float32)
        return lax.optimization_barrier(jnp.sum(rounded_parts, axis=1))
    blocks_out = lax.map(one_block, (context.reshape(BLOCKS, GROUP_TOKENS, HEAD_COUNT * HEAD_WIDTH), adapter_stored_row.reshape(BLOCKS, GROUP_TOKENS)))
    return blocks_out.reshape(TOKENS, MODEL_WIDTH)

def expert_total(normed, expert_choice_pairs, weight_first, weight_second, expert_gate_weight, expert_up_weight, expert_down_weight):
    rows_all = BLOCKS * CAP
    span_width = FF // N_TP
    token_range = jnp.arange(TOKENS, dtype=jnp.int32)
    block_of = token_range // GROUP_TOKENS
    moe_total = jnp.zeros((TOKENS, MODEL_WIDTH), jnp.float32)
    for expert in range(EXPERTS):
        first_hit = expert_choice_pairs[:, 0] == expert
        second_hit = expert_choice_pairs[:, 1] == expert
        chosen = first_hit | second_hit
        counted = jnp.cumsum(chosen.astype(jnp.int32).reshape(BLOCKS, GROUP_TOKENS), axis=1).reshape(TOKENS) - 1
        target_row = jnp.where(chosen, block_of * CAP + counted, rows_all).astype(jnp.int32)
        source_row = jnp.zeros((rows_all + 1,), jnp.int32).at[target_row].set(token_range)
        routed_rows = normed[source_row[:rows_all]].reshape(BLOCKS, COPIES, QUOTA, MODEL_WIDTH)
        out_parts = []
        for copy in range(COPIES):
            holder = copy * EXPERTS + expert
            rows_copy = routed_rows[:, copy].reshape(BLOCKS * QUOTA, MODEL_WIDTH)
            gate_value = jnp.dot(rows_copy, expert_gate_weight[holder], preferred_element_type=jnp.float32)
            up_value = jnp.dot(rows_copy, expert_up_weight[holder], preferred_element_type=jnp.float32)
            hidden = (jax.nn.silu(gate_value) * up_value).astype(jnp.bfloat16)
            hid_spans = jnp.transpose(hidden.reshape(BLOCKS * QUOTA, N_TP, span_width), (1, 0, 2))
            down_spans = expert_down_weight[holder].reshape(N_TP, span_width, MODEL_WIDTH)

            def add_span(running, span_pair):
                span_term = jnp.dot(span_pair[0], span_pair[1], preferred_element_type=jnp.float32)
                return (running + lax.optimization_barrier(span_term.astype(jnp.bfloat16)).astype(jnp.float32), None)
            copy_out, ignored = lax.scan(add_span, jnp.zeros((BLOCKS * QUOTA, MODEL_WIDTH), jnp.float32), (hid_spans, down_spans))
            out_parts.append(copy_out.reshape(BLOCKS, 1, QUOTA, MODEL_WIDTH))
        expert_out = jnp.concatenate(out_parts, axis=1).reshape(rows_all, MODEL_WIDTH)
        padded_out = jnp.concatenate([expert_out, jnp.zeros((1, MODEL_WIDTH), jnp.float32)], axis=0)
        token_out = padded_out[target_row]
        token_weight = jnp.where(first_hit, weight_first, 0.0) + jnp.where(second_hit, weight_second, 0.0)
        moe_total = moe_total + token_weight[:, None] * token_out
    return moe_total

def reference(residual, context, attention_output_weight, adapter_down_maps, adapter_up_maps, adapter_storage_row, active_adapters, request_token_length, request_adapter_entry, expert_norm_gain, router_projection, expert_choice_pairs, expert_gate_weight, expert_up_weight, expert_down_weight):
    pick_tok = token_picks(request_token_length, request_adapter_entry).reshape(TOKENS)
    adapter_stored_row = adapter_storage_row[active_adapters[pick_tok]].astype(jnp.int32)
    blended_rows = residual.astype(jnp.float32) + head_feature_total(context, attention_output_weight, adapter_down_maps, adapter_up_maps, adapter_stored_row)
    mean_square = lax.optimization_barrier(jnp.mean(blended_rows * blended_rows, axis=1, keepdims=True))
    normed = (blended_rows * lax.rsqrt(mean_square + NORM_EPS) * expert_norm_gain.astype(jnp.float32)).astype(jnp.bfloat16)
    logits = jnp.dot(normed, router_projection, preferred_element_type=jnp.float32)
    logit_first = jnp.take_along_axis(logits, expert_choice_pairs[:, 0:1].astype(jnp.int32), axis=1)[:, 0]
    logit_second = jnp.take_along_axis(logits, expert_choice_pairs[:, 1:2].astype(jnp.int32), axis=1)[:, 0]
    weight_first = 1.0 / (1.0 + jnp.exp(logit_second - logit_first))
    weight_second = 1.0 / (1.0 + jnp.exp(logit_first - logit_second))
    moe_total = expert_total(normed, expert_choice_pairs, weight_first, weight_second, expert_gate_weight, expert_up_weight, expert_down_weight)
    return (blended_rows + moe_total).astype(jnp.bfloat16)
```

```python
import jax
import jax.numpy as jnp
from jax import lax
from jax.sharding import Mesh
from jax.sharding import PartitionSpec as P

CAP = 80


NORM_EPS = 1e-05

REQ = ("ry", "rxz")


def segment_onehot(request_token_length, token_count):
    bounds = jnp.cumsum(request_token_length[0])
    position = jnp.arange(token_count, dtype=jnp.int32)
    segment = jnp.sum((position[:, None] >= bounds[None, :]).astype(jnp.int32), axis=1)
    slot_range = jnp.arange(request_token_length.shape[1], dtype=jnp.int32)
    return segment[:, None] == slot_range[None, :]


def route_tables(expert_choice_pairs, expert_count, capacity):
    expert_ids = jnp.arange(expert_count, dtype=jnp.int32)
    first_hit = expert_choice_pairs[None, :, 0] == expert_ids[:, None]
    second_hit = expert_choice_pairs[None, :, 1] == expert_ids[:, None]
    chosen = first_hit | second_hit
    slot_of = jnp.cumsum(chosen.astype(jnp.int32), axis=1) - 1
    slot_range = jnp.arange(capacity, dtype=jnp.int32)
    placement = chosen[:, None, :] & (slot_of[:, None, :] == slot_range[None, :, None])
    return (placement, first_hit, second_hit)


def on_device(
    residual,
    context,
    attention_output_weight,
    adapter_down_maps,
    adapter_up_maps,
    adapter_storage_row,
    active_adapters,
    request_token_length,
    request_adapter_entry,
    expert_norm_gain,
    router_projection,
    expert_choice_pairs,
    expert_gate_weight,
    expert_up_weight,
    expert_down_weight,
):
    token_count = residual.shape[0]
    hidden_width = residual.shape[1]
    feature_share = context.shape[1]
    local_rows = adapter_down_maps.shape[0]
    adapter_rank_size = adapter_down_maps.shape[2]
    request_count = request_token_length.shape[1]
    share_width = hidden_width // lax.axis_size("tp")
    share_start = lax.axis_index("tp") * share_width

    up_slice = lax.dynamic_slice_in_dim(adapter_up_maps, share_start, share_width, 2)
    packed = jnp.concatenate(
        [
            adapter_down_maps.reshape(local_rows, feature_share * adapter_rank_size),
            up_slice.reshape(local_rows, adapter_rank_size * share_width),
        ],
        axis=1,
    )
    all_packed = lax.all_gather(packed, REQ, axis=0, tiled=True)
    request_rows = adapter_storage_row[active_adapters[request_adapter_entry[0]]]
    picked = all_packed[request_rows]
    down_req = picked[:, : feature_share * adapter_rank_size].reshape(
        request_count, feature_share, adapter_rank_size
    )
    up_req = picked[:, feature_share * adapter_rank_size :].reshape(
        request_count * adapter_rank_size, share_width
    )
    down_joined = jnp.transpose(down_req, (1, 0, 2)).reshape(
        feature_share, request_count * adapter_rank_size
    )
    segment_hot = segment_onehot(request_token_length, token_count)
    low_all = jnp.dot(context, down_joined, preferred_element_type=jnp.float32)
    reduced_mask = jnp.repeat(segment_hot, adapter_rank_size, axis=1)
    low_part = jnp.where(reduced_mask, low_all, 0.0)
    low_total = lax.psum(low_part, "tp").astype(jnp.bfloat16)
    lora_share = jnp.dot(low_total, up_req, preferred_element_type=jnp.float32)

    base = jnp.dot(context, attention_output_weight, preferred_element_type=jnp.float32)
    base_share = lax.dynamic_slice_in_dim(base, share_start, share_width, 1)
    head_part = lax.dynamic_update_slice_in_dim(base, base_share + lora_share, share_start, 1)
    gain_all = expert_norm_gain.astype(jnp.float32)
    head_sum = lax.psum(head_part.astype(jnp.bfloat16), "tp").astype(jnp.float32)
    blended_rows = residual.astype(jnp.float32) + head_sum
    mean_square = jnp.mean(blended_rows * blended_rows, axis=1, keepdims=True)
    normed = (blended_rows * lax.rsqrt(mean_square + NORM_EPS) * gain_all).astype(jnp.bfloat16)
    mixed_share = lax.dynamic_slice_in_dim(blended_rows, share_start, share_width, 1)
    logits = jnp.dot(normed, router_projection, preferred_element_type=jnp.float32)
    expert_count = router_projection.shape[1]
    expert_range = jnp.arange(expert_count, dtype=jnp.int32)
    logit_first = jnp.sum(
        jnp.where(expert_choice_pairs[:, 0:1] == expert_range[None, :], logits, 0.0), axis=1
    )
    logit_second = jnp.sum(
        jnp.where(expert_choice_pairs[:, 1:2] == expert_range[None, :], logits, 0.0), axis=1
    )
    weight_first = 1.0 / (1.0 + jnp.exp(logit_second - logit_first))
    weight_second = 1.0 / (1.0 + jnp.exp(logit_first - logit_second))

    placement, first_hit, second_hit = route_tables(expert_choice_pairs, expert_count, CAP)
    send_rows = jnp.einsum(
        "est,td->esd", placement.astype(jnp.bfloat16), normed, preferred_element_type=jnp.float32
    ).astype(jnp.bfloat16)
    rows_in = lax.all_to_all(send_rows, "rxz", split_axis=0, concat_axis=0, tiled=True)
    rows_flat = rows_in.reshape(expert_count * CAP, hidden_width)
    gate_value = jnp.dot(rows_flat, expert_gate_weight[0], preferred_element_type=jnp.float32)
    up_value = jnp.dot(rows_flat, expert_up_weight[0], preferred_element_type=jnp.float32)
    hidden = (jax.nn.silu(gate_value) * up_value).astype(jnp.bfloat16)
    partial_value = jnp.dot(hidden, expert_down_weight[0], preferred_element_type=jnp.float32)
    returned = lax.all_to_all(
        partial_value.astype(jnp.bfloat16).reshape(expert_count, CAP, hidden_width),
        "rxz",
        split_axis=0,
        concat_axis=0,
        tiled=True,
    )
    token_weight = jnp.where(first_hit, weight_first[None, :], 0.0) + jnp.where(
        second_hit, weight_second[None, :], 0.0
    )
    scaled_place = placement.astype(jnp.float32) * token_weight[:, None, :]
    contribution = jnp.einsum(
        "est,esd->td",
        scaled_place,
        returned.astype(jnp.float32),
        precision=lax.Precision.HIGHEST,
        preferred_element_type=jnp.float32,
    )
    moe_share = lax.psum_scatter(
        contribution.astype(jnp.bfloat16), "tp", scatter_dimension=1, tiled=True
    ).astype(jnp.float32)
    return (mixed_share + moe_share).astype(jnp.bfloat16)


def solution(mesh):
    req_size = mesh.shape["req"]
    plane = 8
    split_mesh = Mesh(
        mesh.devices.reshape(req_size // plane, plane, mesh.shape["tp"]), ("ry", "rxz", "tp")
    )
    return jax.shard_map(
        on_device,
        mesh=split_mesh,
        in_specs=(
            P(REQ, None),
            P(REQ, "tp"),
            P("tp", None),
            P(REQ, "tp", None),
            P(REQ, None, None),
            P(),
            P(),
            P(REQ, None),
            P(REQ, None),
            P(),
            P(),
            P(REQ, None),
            P(REQ, None, "tp"),
            P(REQ, None, "tp"),
            P(REQ, "tp", None),
        ),
        out_specs=P(REQ, "tp"),
        check_vma=False,
    )
```

```python
import jax
import jax.numpy as jnp
from jax import lax
from jax.sharding import Mesh
from jax.sharding import PartitionSpec as P

CAP = 80


NORM_EPS = 1e-05

REQ = ("ry", "rxz")
TP = ("tz", "tc")
PAIR = [(0, 1), (1, 0)]


def segment_onehot(request_token_length, token_count):
    bounds = jnp.cumsum(request_token_length[0])
    position = jnp.arange(token_count, dtype=jnp.int32)
    segment = jnp.sum((position[:, None] >= bounds[None, :]).astype(jnp.int32), axis=1)
    slot_range = jnp.arange(request_token_length.shape[1], dtype=jnp.int32)
    return segment[:, None] == slot_range[None, :]


def route_tables(expert_choice_pairs, expert_count, capacity):
    expert_ids = jnp.arange(expert_count, dtype=jnp.int32)
    first_hit = expert_choice_pairs[None, :, 0] == expert_ids[:, None]
    second_hit = expert_choice_pairs[None, :, 1] == expert_ids[:, None]
    chosen = first_hit | second_hit
    slot_of = jnp.cumsum(chosen.astype(jnp.int32), axis=1) - 1
    slot_range = jnp.arange(capacity, dtype=jnp.int32)
    placement = chosen[:, None, :] & (slot_of[:, None, :] == slot_range[None, :, None])
    return (placement, first_hit, second_hit)


def pair_psum(value, share_width):
    rows = value.shape[0]
    chip_count = lax.axis_size("tz")
    core = lax.axis_index("tc")
    split = value.reshape(rows, chip_count, 2, share_width)
    keep = lax.dynamic_index_in_dim(split, core, 2, keepdims=False)
    give = lax.dynamic_index_in_dim(split, 1 - core, 2, keepdims=False)
    got = lax.ppermute(give, "tc", PAIR)
    pair = (keep.astype(jnp.float32) + got.astype(jnp.float32)).astype(value.dtype)
    chips = lax.psum(pair, "tz")
    other = lax.ppermute(chips, "tc", PAIR)
    joined = jnp.where(
        core == 0,
        jnp.stack([chips, other], axis=2),
        jnp.stack([other, chips], axis=2),
    )
    return joined.reshape(value.shape)


def on_device(
    residual,
    context,
    attention_output_weight,
    adapter_down_maps,
    adapter_up_maps,
    adapter_storage_row,
    active_adapters,
    request_token_length,
    request_adapter_entry,
    expert_norm_gain,
    router_projection,
    expert_choice_pairs,
    expert_gate_weight,
    expert_up_weight,
    expert_down_weight,
):
    token_count = residual.shape[0]
    hidden_width = residual.shape[1]
    feature_share = context.shape[1]
    local_rows = adapter_down_maps.shape[0]
    adapter_rank_size = adapter_down_maps.shape[2]
    request_count = request_token_length.shape[1]
    share_width = hidden_width // (lax.axis_size("tz") * 2)
    share_start = (lax.axis_index("tz") * 2 + lax.axis_index("tc")) * share_width

    up_slice = lax.dynamic_slice_in_dim(adapter_up_maps, share_start, share_width, 2)
    packed = jnp.concatenate(
        [
            adapter_down_maps.reshape(local_rows, feature_share * adapter_rank_size),
            up_slice.reshape(local_rows, adapter_rank_size * share_width),
        ],
        axis=1,
    )
    all_packed = lax.all_gather(packed, REQ, axis=0, tiled=True)
    request_rows = adapter_storage_row[active_adapters[request_adapter_entry[0]]]
    picked = all_packed[request_rows]
    down_req = picked[:, : feature_share * adapter_rank_size].reshape(
        request_count, feature_share, adapter_rank_size
    )
    up_req = picked[:, feature_share * adapter_rank_size :].reshape(
        request_count * adapter_rank_size, share_width
    )
    down_joined = jnp.transpose(down_req, (1, 0, 2)).reshape(
        feature_share, request_count * adapter_rank_size
    )
    segment_hot = segment_onehot(request_token_length, token_count)
    low_all = jnp.dot(context, down_joined, preferred_element_type=jnp.float32)
    reduced_mask = jnp.repeat(segment_hot, adapter_rank_size, axis=1)
    low_part = jnp.where(reduced_mask, low_all, 0.0)
    low_total = lax.psum(low_part, TP).astype(jnp.bfloat16)
    lora_share = jnp.dot(low_total, up_req, preferred_element_type=jnp.float32)

    base = jnp.dot(context, attention_output_weight, preferred_element_type=jnp.float32)
    base_share = lax.dynamic_slice_in_dim(base, share_start, share_width, 1)
    head_part = lax.dynamic_update_slice_in_dim(base, base_share + lora_share, share_start, 1)
    gain_all = expert_norm_gain.astype(jnp.float32)
    head_sum = pair_psum(head_part.astype(jnp.bfloat16), share_width).astype(jnp.float32)
    blended_rows = residual.astype(jnp.float32) + head_sum
    mean_square = jnp.mean(blended_rows * blended_rows, axis=1, keepdims=True)
    normed = (blended_rows * lax.rsqrt(mean_square + NORM_EPS) * gain_all).astype(jnp.bfloat16)
    mixed_share = lax.dynamic_slice_in_dim(blended_rows, share_start, share_width, 1)
    logits = jnp.dot(normed, router_projection, preferred_element_type=jnp.float32)
    expert_count = router_projection.shape[1]
    expert_range = jnp.arange(expert_count, dtype=jnp.int32)
    logit_first = jnp.sum(
        jnp.where(expert_choice_pairs[:, 0:1] == expert_range[None, :], logits, 0.0), axis=1
    )
    logit_second = jnp.sum(
        jnp.where(expert_choice_pairs[:, 1:2] == expert_range[None, :], logits, 0.0), axis=1
    )
    weight_first = 1.0 / (1.0 + jnp.exp(logit_second - logit_first))
    weight_second = 1.0 / (1.0 + jnp.exp(logit_first - logit_second))

    placement, first_hit, second_hit = route_tables(expert_choice_pairs, expert_count, CAP)
    send_rows = jnp.einsum(
        "est,td->esd", placement.astype(jnp.bfloat16), normed, preferred_element_type=jnp.float32
    ).astype(jnp.bfloat16)
    send_halves = send_rows.reshape(expert_count, CAP, 2, hidden_width // 2)
    core = lax.axis_index("tc")
    own_half = lax.dynamic_index_in_dim(send_halves, core, 2, keepdims=False)
    half_in = lax.all_to_all(own_half, "rxz", split_axis=0, concat_axis=0, tiled=True)
    other_in = lax.ppermute(half_in, "tc", PAIR)
    rows_in = jnp.where(
        core == 0,
        jnp.concatenate([half_in, other_in], axis=2),
        jnp.concatenate([other_in, half_in], axis=2),
    )
    rows_flat = rows_in.reshape(expert_count * CAP, hidden_width)
    gate_value = jnp.dot(rows_flat, expert_gate_weight[0], preferred_element_type=jnp.float32)
    up_value = jnp.dot(rows_flat, expert_up_weight[0], preferred_element_type=jnp.float32)
    hidden = (jax.nn.silu(gate_value) * up_value).astype(jnp.bfloat16)
    partial_value = jnp.dot(hidden, expert_down_weight[0], preferred_element_type=jnp.float32)
    chip_count = lax.axis_size("tz")
    partial_split = partial_value.astype(jnp.bfloat16).reshape(
        expert_count * CAP, chip_count, 2, share_width
    )
    keep_part = lax.dynamic_index_in_dim(partial_split, core, 2, keepdims=False)
    give_part = lax.dynamic_index_in_dim(partial_split, 1 - core, 2, keepdims=False)
    got_part = lax.ppermute(give_part, "tc", PAIR)
    pair_value = (keep_part.astype(jnp.float32) + got_part.astype(jnp.float32)).astype(jnp.bfloat16)
    returned = lax.all_to_all(
        pair_value.reshape(expert_count, CAP, chip_count * share_width),
        "rxz",
        split_axis=0,
        concat_axis=0,
        tiled=True,
    )
    token_weight = jnp.where(first_hit, weight_first[None, :], 0.0) + jnp.where(
        second_hit, weight_second[None, :], 0.0
    )
    scaled_place = placement.astype(jnp.float32) * token_weight[:, None, :]
    contribution = jnp.einsum(
        "est,esd->td",
        scaled_place,
        returned.astype(jnp.float32),
        precision=lax.Precision.HIGHEST,
        preferred_element_type=jnp.float32,
    )
    moe_share = lax.psum_scatter(
        contribution.astype(jnp.bfloat16), "tz", scatter_dimension=1, tiled=True
    ).astype(jnp.float32)
    return (mixed_share + moe_share).astype(jnp.bfloat16)


def solution(mesh):
    req_size = mesh.shape["req"]
    plane = 8
    split_mesh = Mesh(
        mesh.devices.reshape(req_size // plane, plane, mesh.shape["tp"] // 2, 2),
        ("ry", "rxz", "tz", "tc"),
    )
    return jax.shard_map(
        on_device,
        mesh=split_mesh,
        in_specs=(
            P(REQ, None),
            P(REQ, TP),
            P(TP, None),
            P(REQ, TP, None),
            P(REQ, None, None),
            P(),
            P(),
            P(REQ, None),
            P(REQ, None),
            P(),
            P(),
            P(REQ, None),
            P(REQ, None, TP),
            P(REQ, None, TP),
            P(REQ, TP, None),
        ),
        out_specs=P(REQ, TP),
        check_vma=False,
    )
```

```python
import jax
import jax.numpy as jnp
from jax import lax
from jax.sharding import Mesh
from jax.sharding import PartitionSpec as P

CAP = 80


NORM_EPS = 1e-05

REQ = ("ry", "rxz")
TP = ("tz", "tc")
PAIR = [(0, 1), (1, 0)]


def segment_onehot(request_token_length, token_count):
    bounds = jnp.cumsum(request_token_length[0])
    position = jnp.arange(token_count, dtype=jnp.int32)
    segment = jnp.sum((position[:, None] >= bounds[None, :]).astype(jnp.int32), axis=1)
    slot_range = jnp.arange(request_token_length.shape[1], dtype=jnp.int32)
    return segment[:, None] == slot_range[None, :]


def route_tables(expert_choice_pairs, expert_count, capacity):
    expert_ids = jnp.arange(expert_count, dtype=jnp.int32)
    first_hit = expert_choice_pairs[None, :, 0] == expert_ids[:, None]
    second_hit = expert_choice_pairs[None, :, 1] == expert_ids[:, None]
    chosen = first_hit | second_hit
    slot_of = jnp.cumsum(chosen.astype(jnp.int32), axis=1) - 1
    slot_range = jnp.arange(capacity, dtype=jnp.int32)
    placement = chosen[:, None, :] & (slot_of[:, None, :] == slot_range[None, :, None])
    return (placement, first_hit, second_hit)


def shift_pairs(size, step):
    return [(source, (source + step) % size) for source in range(size)]


def chip_reduce_scatter(chunks):
    count = chunks.shape[0]
    place = lax.axis_index("tz")
    total = lax.dynamic_index_in_dim(chunks, place, 0, keepdims=False).astype(jnp.float32)
    for step in range(1, count):
        give = lax.dynamic_index_in_dim(chunks, (place + step) % count, 0, keepdims=False)
        total = total + lax.ppermute(give, "tz", shift_pairs(count, step)).astype(jnp.float32)
    return total


def tp_all_gather(piece, count):
    place = lax.axis_index("tz") * 2 + lax.axis_index("tc")
    got = [piece]
    for step in range(1, count):
        got.append(lax.ppermute(piece, TP, shift_pairs(count, step)))
    stacked = jnp.stack(got, axis=0)
    order = (place - jnp.arange(count, dtype=jnp.int32)) % count
    return jnp.take(stacked, order, axis=0)


def tp_psum(value, count):
    total = value
    for step in range(1, count):
        total = total + lax.ppermute(value, TP, shift_pairs(count, step))
    return total


def pair_psum(value, share_width):
    rows = value.shape[0]
    chip_count = lax.axis_size("tz")
    core = lax.axis_index("tc")
    split = value.reshape(rows, chip_count, 2, share_width)
    keep = lax.dynamic_index_in_dim(split, core, 2, keepdims=False)
    give = lax.dynamic_index_in_dim(split, 1 - core, 2, keepdims=False)
    got = lax.ppermute(give, "tc", PAIR)
    pair = (keep.astype(jnp.float32) + got.astype(jnp.float32)).astype(value.dtype)
    own = chip_reduce_scatter(jnp.transpose(pair, (1, 0, 2))).astype(value.dtype)
    every = tp_all_gather(own, chip_count * 2)
    return jnp.transpose(every, (1, 0, 2)).reshape(value.shape)


def on_device(
    residual,
    context,
    attention_output_weight,
    adapter_down_maps,
    adapter_up_maps,
    adapter_storage_row,
    active_adapters,
    request_token_length,
    request_adapter_entry,
    expert_norm_gain,
    router_projection,
    expert_choice_pairs,
    expert_gate_weight,
    expert_up_weight,
    expert_down_weight,
):
    token_count = residual.shape[0]
    hidden_width = residual.shape[1]
    feature_share = context.shape[1]
    local_rows = adapter_down_maps.shape[0]
    adapter_rank_size = adapter_down_maps.shape[2]
    request_count = request_token_length.shape[1]
    share_width = hidden_width // (lax.axis_size("tz") * 2)
    share_start = (lax.axis_index("tz") * 2 + lax.axis_index("tc")) * share_width

    up_slice = lax.dynamic_slice_in_dim(adapter_up_maps, share_start, share_width, 2)
    packed = jnp.concatenate(
        [
            adapter_down_maps.reshape(local_rows, feature_share * adapter_rank_size),
            up_slice.reshape(local_rows, adapter_rank_size * share_width),
        ],
        axis=1,
    )
    req_count = lax.axis_size("ry") * lax.axis_size("rxz")
    all_packed = lax.all_to_all(
        jnp.broadcast_to(packed[None], (req_count,) + packed.shape),
        REQ,
        split_axis=0,
        concat_axis=0,
        tiled=True,
    ).reshape(req_count * local_rows, packed.shape[1])
    request_rows = adapter_storage_row[active_adapters[request_adapter_entry[0]]]
    picked = all_packed[request_rows]
    down_req = picked[:, : feature_share * adapter_rank_size].reshape(
        request_count, feature_share, adapter_rank_size
    )
    up_req = picked[:, feature_share * adapter_rank_size :].reshape(
        request_count * adapter_rank_size, share_width
    )
    down_joined = jnp.transpose(down_req, (1, 0, 2)).reshape(
        feature_share, request_count * adapter_rank_size
    )
    segment_hot = segment_onehot(request_token_length, token_count)
    low_all = jnp.dot(context, down_joined, preferred_element_type=jnp.float32)
    reduced_mask = jnp.repeat(segment_hot, adapter_rank_size, axis=1)
    low_part = jnp.where(reduced_mask, low_all, 0.0)
    low_total = tp_psum(low_part, lax.axis_size("tz") * 2).astype(jnp.bfloat16)
    lora_share = jnp.dot(low_total, up_req, preferred_element_type=jnp.float32)

    base = jnp.dot(context, attention_output_weight, preferred_element_type=jnp.float32)
    base_share = lax.dynamic_slice_in_dim(base, share_start, share_width, 1)
    head_part = lax.dynamic_update_slice_in_dim(base, base_share + lora_share, share_start, 1)
    gain_all = expert_norm_gain.astype(jnp.float32)
    head_sum = pair_psum(head_part.astype(jnp.bfloat16), share_width).astype(jnp.float32)
    blended_rows = residual.astype(jnp.float32) + head_sum
    mean_square = jnp.mean(blended_rows * blended_rows, axis=1, keepdims=True)
    normed = (blended_rows * lax.rsqrt(mean_square + NORM_EPS) * gain_all).astype(jnp.bfloat16)
    mixed_share = lax.dynamic_slice_in_dim(blended_rows, share_start, share_width, 1)
    logits = jnp.dot(normed, router_projection, preferred_element_type=jnp.float32)
    expert_count = router_projection.shape[1]
    expert_range = jnp.arange(expert_count, dtype=jnp.int32)
    logit_first = jnp.sum(
        jnp.where(expert_choice_pairs[:, 0:1] == expert_range[None, :], logits, 0.0), axis=1
    )
    logit_second = jnp.sum(
        jnp.where(expert_choice_pairs[:, 1:2] == expert_range[None, :], logits, 0.0), axis=1
    )
    weight_first = 1.0 / (1.0 + jnp.exp(logit_second - logit_first))
    weight_second = 1.0 / (1.0 + jnp.exp(logit_first - logit_second))

    placement, first_hit, second_hit = route_tables(expert_choice_pairs, expert_count, CAP)
    send_rows = jnp.einsum(
        "est,td->esd", placement.astype(jnp.bfloat16), normed, preferred_element_type=jnp.float32
    ).astype(jnp.bfloat16)
    send_halves = send_rows.reshape(expert_count, CAP, 2, hidden_width // 2)
    core = lax.axis_index("tc")
    own_half = lax.dynamic_index_in_dim(send_halves, core, 2, keepdims=False)
    half_in = lax.all_to_all(own_half, "rxz", split_axis=0, concat_axis=0, tiled=True)
    other_in = lax.ppermute(half_in, "tc", PAIR)
    rows_in = jnp.where(
        core == 0,
        jnp.concatenate([half_in, other_in], axis=2),
        jnp.concatenate([other_in, half_in], axis=2),
    )
    rows_flat = rows_in.reshape(expert_count * CAP, hidden_width)
    gate_value = jnp.dot(rows_flat, expert_gate_weight[0], preferred_element_type=jnp.float32)
    up_value = jnp.dot(rows_flat, expert_up_weight[0], preferred_element_type=jnp.float32)
    hidden = (jax.nn.silu(gate_value) * up_value).astype(jnp.bfloat16)
    partial_value = jnp.dot(hidden, expert_down_weight[0], preferred_element_type=jnp.float32)
    chip_count = lax.axis_size("tz")
    partial_split = partial_value.astype(jnp.bfloat16).reshape(
        expert_count * CAP, chip_count, 2, share_width
    )
    keep_part = lax.dynamic_index_in_dim(partial_split, core, 2, keepdims=False)
    give_part = lax.dynamic_index_in_dim(partial_split, 1 - core, 2, keepdims=False)
    got_part = lax.ppermute(give_part, "tc", PAIR)
    pair_value = (keep_part.astype(jnp.float32) + got_part.astype(jnp.float32)).astype(jnp.bfloat16)
    returned = lax.all_to_all(
        pair_value.reshape(expert_count, CAP, chip_count * share_width),
        "rxz",
        split_axis=0,
        concat_axis=0,
        tiled=True,
    )
    token_weight = jnp.where(first_hit, weight_first[None, :], 0.0) + jnp.where(
        second_hit, weight_second[None, :], 0.0
    )
    scaled_place = placement.astype(jnp.float32) * token_weight[:, None, :]
    contribution = jnp.einsum(
        "est,esd->td",
        scaled_place,
        returned.astype(jnp.float32),
        precision=lax.Precision.HIGHEST,
        preferred_element_type=jnp.float32,
    )
    moe_chunks = jnp.transpose(
        contribution.astype(jnp.bfloat16).reshape(token_count, chip_count, share_width), (1, 0, 2)
    )
    moe_share = chip_reduce_scatter(moe_chunks)
    return (mixed_share + moe_share).astype(jnp.bfloat16)


def solution(mesh):
    req_size = mesh.shape["req"]
    plane = 8
    split_mesh = Mesh(
        mesh.devices.reshape(req_size // plane, plane, mesh.shape["tp"] // 2, 2),
        ("ry", "rxz", "tz", "tc"),
    )
    return jax.shard_map(
        on_device,
        mesh=split_mesh,
        in_specs=(
            P(REQ, None),
            P(REQ, TP),
            P(TP, None),
            P(REQ, TP, None),
            P(REQ, None, None),
            P(),
            P(),
            P(REQ, None),
            P(REQ, None),
            P(),
            P(),
            P(REQ, None),
            P(REQ, None, TP),
            P(REQ, None, TP),
            P(REQ, TP, None),
        ),
        out_specs=P(REQ, TP),
        check_vma=False,
    )
```

```python
import jax
import jax.numpy as jnp
from jax import lax
from jax.sharding import Mesh
from jax.sharding import PartitionSpec as P

CAP = 80


NORM_EPS = 1e-05

REQ = ("ry", "rxz")
TP = ("tz", "tc")
PAIR = [(0, 1), (1, 0)]


def segment_onehot(request_token_length, token_count):
    bounds = jnp.cumsum(request_token_length[0])
    position = jnp.arange(token_count, dtype=jnp.int32)
    segment = jnp.sum((position[:, None] >= bounds[None, :]).astype(jnp.int32), axis=1)
    slot_range = jnp.arange(request_token_length.shape[1], dtype=jnp.int32)
    return segment[:, None] == slot_range[None, :]


def route_tables(expert_choice_pairs, expert_count, capacity):
    expert_ids = jnp.arange(expert_count, dtype=jnp.int32)
    first_hit = expert_choice_pairs[None, :, 0] == expert_ids[:, None]
    second_hit = expert_choice_pairs[None, :, 1] == expert_ids[:, None]
    chosen = first_hit | second_hit
    slot_of = jnp.cumsum(chosen.astype(jnp.int32), axis=1) - 1
    slot_range = jnp.arange(capacity, dtype=jnp.int32)
    placement = chosen[:, None, :] & (slot_of[:, None, :] == slot_range[None, :, None])
    return (placement, first_hit, second_hit)


def shift_pairs(size, step):
    return [(source, (source + step) % size) for source in range(size)]


def chip_reduce_scatter(chunks):
    count = chunks.shape[0]
    place = lax.axis_index("tz")
    total = lax.dynamic_index_in_dim(chunks, place, 0, keepdims=False).astype(jnp.float32)
    for step in range(1, count):
        give = lax.dynamic_index_in_dim(chunks, (place + step) % count, 0, keepdims=False)
        total = total + lax.ppermute(give, "tz", shift_pairs(count, step)).astype(jnp.float32)
    return total


def tp_all_gather(piece, count):
    place = lax.axis_index("tz") * 2 + lax.axis_index("tc")
    got = [piece]
    for step in range(1, count):
        got.append(lax.ppermute(piece, TP, shift_pairs(count, step)))
    stacked = jnp.stack(got, axis=0)
    order = (place - jnp.arange(count, dtype=jnp.int32)) % count
    return jnp.take(stacked, order, axis=0)


def tp_psum(value, count):
    total = value
    for step in range(1, count):
        total = total + lax.ppermute(value, TP, shift_pairs(count, step))
    return total


def pair_reduce_scatter(value, share_width):
    rows = value.shape[0]
    chip_count = lax.axis_size("tz")
    core = lax.axis_index("tc")
    split = value.reshape(rows, chip_count, 2, share_width)
    keep = lax.dynamic_index_in_dim(split, core, 2, keepdims=False)
    give = lax.dynamic_index_in_dim(split, 1 - core, 2, keepdims=False)
    got = lax.ppermute(give, "tc", PAIR)
    pair = (keep.astype(jnp.float32) + got.astype(jnp.float32)).astype(value.dtype)
    return chip_reduce_scatter(jnp.transpose(pair, (1, 0, 2)))


def on_device(
    residual,
    context,
    attention_output_weight,
    adapter_down_maps,
    adapter_up_maps,
    adapter_storage_row,
    active_adapters,
    request_token_length,
    request_adapter_entry,
    expert_norm_gain,
    router_projection,
    expert_choice_pairs,
    expert_gate_weight,
    expert_up_weight,
    expert_down_weight,
):
    token_count = residual.shape[0]
    hidden_width = residual.shape[1]
    feature_share = context.shape[1]
    local_rows = adapter_down_maps.shape[0]
    adapter_rank_size = adapter_down_maps.shape[2]
    request_count = request_token_length.shape[1]
    share_width = hidden_width // (lax.axis_size("tz") * 2)
    share_start = (lax.axis_index("tz") * 2 + lax.axis_index("tc")) * share_width

    up_slice = lax.dynamic_slice_in_dim(adapter_up_maps, share_start, share_width, 2)
    packed = jnp.concatenate(
        [
            adapter_down_maps.reshape(local_rows, feature_share * adapter_rank_size),
            up_slice.reshape(local_rows, adapter_rank_size * share_width),
        ],
        axis=1,
    )
    req_count = lax.axis_size("ry") * lax.axis_size("rxz")
    all_packed = lax.all_to_all(
        jnp.broadcast_to(packed[None], (req_count,) + packed.shape),
        REQ,
        split_axis=0,
        concat_axis=0,
        tiled=True,
    ).reshape(req_count * local_rows, packed.shape[1])
    request_rows = adapter_storage_row[active_adapters[request_adapter_entry[0]]]
    picked = all_packed[request_rows]
    down_req = picked[:, : feature_share * adapter_rank_size].reshape(
        request_count, feature_share, adapter_rank_size
    )
    up_req = picked[:, feature_share * adapter_rank_size :].reshape(
        request_count * adapter_rank_size, share_width
    )
    down_joined = jnp.transpose(down_req, (1, 0, 2)).reshape(
        feature_share, request_count * adapter_rank_size
    )
    segment_hot = segment_onehot(request_token_length, token_count)
    low_all = jnp.dot(context, down_joined, preferred_element_type=jnp.float32)
    reduced_mask = jnp.repeat(segment_hot, adapter_rank_size, axis=1)
    low_part = jnp.where(reduced_mask, low_all, 0.0)
    low_total = tp_psum(low_part, lax.axis_size("tz") * 2).astype(jnp.bfloat16)
    lora_share = jnp.dot(low_total, up_req, preferred_element_type=jnp.float32)

    base = jnp.dot(context, attention_output_weight, preferred_element_type=jnp.float32)
    base_share = pair_reduce_scatter(base.astype(jnp.bfloat16), share_width)
    own_share = (base_share + lora_share).astype(jnp.bfloat16)
    head_sum = (
        jnp.transpose(tp_all_gather(own_share, lax.axis_size("tz") * 2), (1, 0, 2))
        .reshape(token_count, hidden_width)
        .astype(jnp.float32)
    )
    gain_all = expert_norm_gain.astype(jnp.float32)
    blended_rows = residual.astype(jnp.float32) + head_sum
    mean_square = jnp.mean(blended_rows * blended_rows, axis=1, keepdims=True)
    normed = (blended_rows * lax.rsqrt(mean_square + NORM_EPS) * gain_all).astype(jnp.bfloat16)
    mixed_share = lax.dynamic_slice_in_dim(blended_rows, share_start, share_width, 1)
    logits = jnp.dot(normed, router_projection, preferred_element_type=jnp.float32)
    expert_count = router_projection.shape[1]
    expert_range = jnp.arange(expert_count, dtype=jnp.int32)
    logit_first = jnp.sum(
        jnp.where(expert_choice_pairs[:, 0:1] == expert_range[None, :], logits, 0.0), axis=1
    )
    logit_second = jnp.sum(
        jnp.where(expert_choice_pairs[:, 1:2] == expert_range[None, :], logits, 0.0), axis=1
    )
    weight_first = 1.0 / (1.0 + jnp.exp(logit_second - logit_first))
    weight_second = 1.0 / (1.0 + jnp.exp(logit_first - logit_second))

    placement, first_hit, second_hit = route_tables(expert_choice_pairs, expert_count, CAP)
    send_rows = jnp.einsum(
        "est,td->esd", placement.astype(jnp.bfloat16), normed, preferred_element_type=jnp.float32
    ).astype(jnp.bfloat16)
    send_halves = send_rows.reshape(expert_count, CAP, 2, hidden_width // 2)
    core = lax.axis_index("tc")
    own_half = lax.dynamic_index_in_dim(send_halves, core, 2, keepdims=False)
    half_in = lax.all_to_all(own_half, "rxz", split_axis=0, concat_axis=0, tiled=True)
    other_in = lax.ppermute(half_in, "tc", PAIR)
    rows_in = jnp.where(
        core == 0,
        jnp.concatenate([half_in, other_in], axis=2),
        jnp.concatenate([other_in, half_in], axis=2),
    )
    rows_flat = rows_in.reshape(expert_count * CAP, hidden_width)
    gate_value = jnp.dot(rows_flat, expert_gate_weight[0], preferred_element_type=jnp.float32)
    up_value = jnp.dot(rows_flat, expert_up_weight[0], preferred_element_type=jnp.float32)
    hidden = (jax.nn.silu(gate_value) * up_value).astype(jnp.bfloat16)
    partial_value = jnp.dot(hidden, expert_down_weight[0], preferred_element_type=jnp.float32)
    chip_count = lax.axis_size("tz")
    partial_split = partial_value.astype(jnp.bfloat16).reshape(
        expert_count * CAP, chip_count, 2, share_width
    )
    keep_part = lax.dynamic_index_in_dim(partial_split, core, 2, keepdims=False)
    give_part = lax.dynamic_index_in_dim(partial_split, 1 - core, 2, keepdims=False)
    got_part = lax.ppermute(give_part, "tc", PAIR)
    pair_value = (keep_part.astype(jnp.float32) + got_part.astype(jnp.float32)).astype(jnp.bfloat16)
    returned = lax.all_to_all(
        pair_value.reshape(expert_count, CAP, chip_count * share_width),
        "rxz",
        split_axis=0,
        concat_axis=0,
        tiled=True,
    )
    token_weight = jnp.where(first_hit, weight_first[None, :], 0.0) + jnp.where(
        second_hit, weight_second[None, :], 0.0
    )
    scaled_place = placement.astype(jnp.float32) * token_weight[:, None, :]
    contribution = jnp.einsum(
        "est,esd->td",
        scaled_place,
        returned.astype(jnp.float32),
        precision=lax.Precision.HIGHEST,
        preferred_element_type=jnp.float32,
    )
    moe_chunks = jnp.transpose(
        contribution.astype(jnp.bfloat16).reshape(token_count, chip_count, share_width), (1, 0, 2)
    )
    moe_share = chip_reduce_scatter(moe_chunks)
    return (mixed_share + moe_share).astype(jnp.bfloat16)


def solution(mesh):
    req_size = mesh.shape["req"]
    plane = 8
    split_mesh = Mesh(
        mesh.devices.reshape(req_size // plane, plane, mesh.shape["tp"] // 2, 2),
        ("ry", "rxz", "tz", "tc"),
    )
    return jax.shard_map(
        on_device,
        mesh=split_mesh,
        in_specs=(
            P(REQ, None),
            P(REQ, TP),
            P(TP, None),
            P(REQ, TP, None),
            P(REQ, None, None),
            P(),
            P(),
            P(REQ, None),
            P(REQ, None),
            P(),
            P(),
            P(REQ, None),
            P(REQ, None, TP),
            P(REQ, None, TP),
            P(REQ, TP, None),
        ),
        out_specs=P(REQ, TP),
        check_vma=False,
    )
```

```python
import jax
import jax.numpy as jnp
from jax import lax
from jax.sharding import Mesh
from jax.sharding import PartitionSpec as P

CAP = 80


NORM_EPS = 1e-05

REQ = ("ry", "rxz")
TP = ("tz", "tc")
PAIR = [(0, 1), (1, 0)]


def segment_onehot(request_token_length, token_count):
    bounds = jnp.cumsum(request_token_length[0])
    position = jnp.arange(token_count, dtype=jnp.int32)
    segment = jnp.sum((position[:, None] >= bounds[None, :]).astype(jnp.int32), axis=1)
    slot_range = jnp.arange(request_token_length.shape[1], dtype=jnp.int32)
    return segment[:, None] == slot_range[None, :]


def route_tables(expert_choice_pairs, expert_count, capacity):
    expert_ids = jnp.arange(expert_count, dtype=jnp.int32)
    first_hit = expert_choice_pairs[None, :, 0] == expert_ids[:, None]
    second_hit = expert_choice_pairs[None, :, 1] == expert_ids[:, None]
    chosen = first_hit | second_hit
    slot_of = jnp.cumsum(chosen.astype(jnp.int32), axis=1) - 1
    slot_range = jnp.arange(capacity, dtype=jnp.int32)
    placement = chosen[:, None, :] & (slot_of[:, None, :] == slot_range[None, :, None])
    return (placement, first_hit, second_hit)


def shift_pairs(size, step):
    return [(source, (source + step) % size) for source in range(size)]


def chip_reduce_scatter(chunks):
    count = chunks.shape[0]
    place = lax.axis_index("tz")
    total = lax.dynamic_index_in_dim(chunks, place, 0, keepdims=False).astype(jnp.float32)
    for step in range(1, count):
        give = lax.dynamic_index_in_dim(chunks, (place + step) % count, 0, keepdims=False)
        total = total + lax.ppermute(give, "tz", shift_pairs(count, step)).astype(jnp.float32)
    return total


def tp_all_gather(piece, count):
    place = lax.axis_index("tz") * 2 + lax.axis_index("tc")
    got = [piece]
    for step in range(1, count):
        got.append(lax.ppermute(piece, TP, shift_pairs(count, step)))
    stacked = jnp.stack(got, axis=0)
    order = (place - jnp.arange(count, dtype=jnp.int32)) % count
    return jnp.take(stacked, order, axis=0)


def tp_psum(value, count):
    total = value
    for step in range(1, count):
        total = total + lax.ppermute(value, TP, shift_pairs(count, step))
    return total


def pair_reduce_scatter(value, share_width):
    rows = value.shape[0]
    chip_count = lax.axis_size("tz")
    core = lax.axis_index("tc")
    split = value.reshape(rows, chip_count, 2, share_width)
    keep = lax.dynamic_index_in_dim(split, core, 2, keepdims=False)
    give = lax.dynamic_index_in_dim(split, 1 - core, 2, keepdims=False)
    got = lax.ppermute(give, "tc", PAIR)
    pair = (keep.astype(jnp.float32) + got.astype(jnp.float32)).astype(value.dtype)
    return chip_reduce_scatter(jnp.transpose(pair, (1, 0, 2)))


def on_device(
    residual,
    context,
    attention_output_weight,
    adapter_down_maps,
    adapter_up_maps,
    adapter_storage_row,
    active_adapters,
    request_token_length,
    request_adapter_entry,
    expert_norm_gain,
    router_projection,
    expert_choice_pairs,
    expert_gate_weight,
    expert_up_weight,
    expert_down_weight,
):
    token_count = residual.shape[0]
    hidden_width = residual.shape[1]
    feature_share = context.shape[1]
    local_rows = adapter_down_maps.shape[0]
    adapter_rank_size = adapter_down_maps.shape[2]
    request_count = request_token_length.shape[1]
    share_width = hidden_width // (lax.axis_size("tz") * 2)
    share_start = (lax.axis_index("tz") * 2 + lax.axis_index("tc")) * share_width

    up_slice = lax.dynamic_slice_in_dim(adapter_up_maps, share_start, share_width, 2)
    packed = jnp.concatenate(
        [
            adapter_down_maps.reshape(local_rows, feature_share * adapter_rank_size),
            up_slice.reshape(local_rows, adapter_rank_size * share_width),
        ],
        axis=1,
    )
    req_count = lax.axis_size("ry") * lax.axis_size("rxz")
    all_packed = lax.all_to_all(
        jnp.broadcast_to(packed[None], (req_count,) + packed.shape),
        REQ,
        split_axis=0,
        concat_axis=0,
        tiled=True,
    ).reshape(req_count * local_rows, packed.shape[1])
    request_rows = adapter_storage_row[active_adapters[request_adapter_entry[0]]]
    picked = all_packed[request_rows]
    down_req = picked[:, : feature_share * adapter_rank_size].reshape(
        request_count, feature_share, adapter_rank_size
    )
    up_req = picked[:, feature_share * adapter_rank_size :].reshape(
        request_count * adapter_rank_size, share_width
    )
    down_joined = jnp.transpose(down_req, (1, 0, 2)).reshape(
        feature_share, request_count * adapter_rank_size
    )
    segment_hot = segment_onehot(request_token_length, token_count)
    low_all = jnp.dot(context, down_joined, preferred_element_type=jnp.float32)
    reduced_mask = jnp.repeat(segment_hot, adapter_rank_size, axis=1)
    low_part = jnp.where(reduced_mask, low_all, 0.0)
    low_total = tp_psum(low_part, lax.axis_size("tz") * 2).astype(jnp.bfloat16)
    lora_share = jnp.dot(low_total, up_req, preferred_element_type=jnp.float32)

    base = jnp.dot(context, attention_output_weight, preferred_element_type=jnp.float32)
    base_share = pair_reduce_scatter(base.astype(jnp.bfloat16), share_width)
    own_share = (base_share + lora_share).astype(jnp.bfloat16)
    head_sum = (
        jnp.transpose(tp_all_gather(own_share, lax.axis_size("tz") * 2), (1, 0, 2))
        .reshape(token_count, hidden_width)
        .astype(jnp.float32)
    )
    gain_all = expert_norm_gain.astype(jnp.float32)
    blended_rows = residual.astype(jnp.float32) + head_sum
    mean_square = jnp.mean(blended_rows * blended_rows, axis=1, keepdims=True)
    normed = (blended_rows * lax.rsqrt(mean_square + NORM_EPS) * gain_all).astype(jnp.bfloat16)
    mixed_share = lax.dynamic_slice_in_dim(blended_rows, share_start, share_width, 1)
    logits = jnp.dot(normed, router_projection, preferred_element_type=jnp.float32)
    expert_count = router_projection.shape[1]
    expert_range = jnp.arange(expert_count, dtype=jnp.int32)
    logit_first = jnp.sum(
        jnp.where(expert_choice_pairs[:, 0:1] == expert_range[None, :], logits, 0.0), axis=1
    )
    logit_second = jnp.sum(
        jnp.where(expert_choice_pairs[:, 1:2] == expert_range[None, :], logits, 0.0), axis=1
    )
    weight_first = 1.0 / (1.0 + jnp.exp(logit_second - logit_first))
    weight_second = 1.0 / (1.0 + jnp.exp(logit_first - logit_second))

    placement, first_hit, second_hit = route_tables(expert_choice_pairs, expert_count, CAP)
    send_rows = jnp.einsum(
        "est,td->esd", placement.astype(jnp.bfloat16), normed, preferred_element_type=jnp.float32
    ).astype(jnp.bfloat16)
    send_halves = send_rows.reshape(expert_count, CAP, 2, hidden_width // 2)
    core = lax.axis_index("tc")
    own_half = lax.dynamic_index_in_dim(send_halves, core, 2, keepdims=False)
    half_in = lax.all_to_all(own_half, "rxz", split_axis=0, concat_axis=0, tiled=True)
    other_in = lax.ppermute(half_in, "tc", PAIR)
    rows_in = jnp.where(
        core == 0,
        jnp.concatenate([half_in, other_in], axis=2),
        jnp.concatenate([other_in, half_in], axis=2),
    )
    rows_flat = rows_in.reshape(expert_count * CAP, hidden_width)
    gate_value = jnp.dot(rows_flat, expert_gate_weight[0], preferred_element_type=jnp.float32)
    up_value = jnp.dot(rows_flat, expert_up_weight[0], preferred_element_type=jnp.float32)
    hidden = (jax.nn.silu(gate_value) * up_value).astype(jnp.bfloat16)
    partial_value = jnp.dot(hidden, expert_down_weight[0], preferred_element_type=jnp.float32)
    chip_count = lax.axis_size("tz")
    partial_split = partial_value.astype(jnp.bfloat16).reshape(
        expert_count * CAP, chip_count, 2, share_width
    )
    keep_part = lax.dynamic_index_in_dim(partial_split, core, 2, keepdims=False)
    give_part = lax.dynamic_index_in_dim(partial_split, 1 - core, 2, keepdims=False)
    got_part = lax.ppermute(give_part, "tc", PAIR)
    pair_value = (keep_part.astype(jnp.float32) + got_part.astype(jnp.float32)).astype(jnp.bfloat16)
    slot_value = chip_reduce_scatter(jnp.transpose(pair_value, (1, 0, 2))).astype(jnp.bfloat16)
    returned = lax.all_to_all(
        slot_value.reshape(expert_count, CAP, share_width),
        "rxz",
        split_axis=0,
        concat_axis=0,
        tiled=True,
    )
    token_weight = jnp.where(first_hit, weight_first[None, :], 0.0) + jnp.where(
        second_hit, weight_second[None, :], 0.0
    )
    scaled_place = placement.astype(jnp.float32) * token_weight[:, None, :]
    contribution = jnp.einsum(
        "est,esd->td",
        scaled_place,
        returned.astype(jnp.float32),
        precision=lax.Precision.HIGHEST,
        preferred_element_type=jnp.float32,
    )
    moe_share = contribution
    return (mixed_share + moe_share).astype(jnp.bfloat16)


def solution(mesh):
    req_size = mesh.shape["req"]
    plane = 8
    split_mesh = Mesh(
        mesh.devices.reshape(req_size // plane, plane, mesh.shape["tp"] // 2, 2),
        ("ry", "rxz", "tz", "tc"),
    )
    return jax.shard_map(
        on_device,
        mesh=split_mesh,
        in_specs=(
            P(REQ, None),
            P(REQ, TP),
            P(TP, None),
            P(REQ, TP, None),
            P(REQ, None, None),
            P(),
            P(),
            P(REQ, None),
            P(REQ, None),
            P(),
            P(),
            P(REQ, None),
            P(REQ, None, TP),
            P(REQ, None, TP),
            P(REQ, TP, None),
        ),
        out_specs=P(REQ, TP),
        check_vma=False,
    )
```

```python
import jax
import jax.numpy as jnp
from jax import lax
from jax.sharding import Mesh
from jax.sharding import PartitionSpec as P

CAP = 80


NORM_EPS = 1e-05

REQ = ("ry", "rxz")
TP = ("tz", "tc")
PAIR = [(0, 1), (1, 0)]


def segment_onehot(request_token_length, token_count):
    bounds = jnp.cumsum(request_token_length[0])
    position = jnp.arange(token_count, dtype=jnp.int32)
    segment = jnp.sum((position[:, None] >= bounds[None, :]).astype(jnp.int32), axis=1)
    slot_range = jnp.arange(request_token_length.shape[1], dtype=jnp.int32)
    return segment[:, None] == slot_range[None, :]


def route_tables(expert_choice_pairs, expert_count, capacity):
    expert_ids = jnp.arange(expert_count, dtype=jnp.int32)
    first_hit = expert_choice_pairs[None, :, 0] == expert_ids[:, None]
    second_hit = expert_choice_pairs[None, :, 1] == expert_ids[:, None]
    chosen = first_hit | second_hit
    slot_of = jnp.cumsum(chosen.astype(jnp.int32), axis=1) - 1
    slot_range = jnp.arange(capacity, dtype=jnp.int32)
    placement = chosen[:, None, :] & (slot_of[:, None, :] == slot_range[None, :, None])
    return (placement, first_hit, second_hit)


def shift_pairs(size, step):
    return [(source, (source + step) % size) for source in range(size)]


def chip_reduce_scatter(chunks):
    count = chunks.shape[0]
    place = lax.axis_index("tz")
    total = lax.dynamic_index_in_dim(chunks, place, 0, keepdims=False).astype(jnp.float32)
    for step in range(1, count):
        give = lax.dynamic_index_in_dim(chunks, (place + step) % count, 0, keepdims=False)
        total = total + lax.ppermute(give, "tz", shift_pairs(count, step)).astype(jnp.float32)
    return total


def tp_all_gather(piece, count):
    place = lax.axis_index("tz") * 2 + lax.axis_index("tc")
    got = [piece]
    for step in range(1, count):
        got.append(lax.ppermute(piece, TP, shift_pairs(count, step)))
    stacked = jnp.stack(got, axis=0)
    order = (place - jnp.arange(count, dtype=jnp.int32)) % count
    return jnp.take(stacked, order, axis=0)


def tp_psum(value, count):
    total = value
    for step in range(1, count):
        total = total + lax.ppermute(value, TP, shift_pairs(count, step))
    return total


def pair_reduce_scatter(value, share_width):
    rows = value.shape[0]
    chip_count = lax.axis_size("tz")
    core = lax.axis_index("tc")
    split = value.reshape(rows, chip_count, 2, share_width)
    keep = lax.dynamic_index_in_dim(split, core, 2, keepdims=False)
    give = lax.dynamic_index_in_dim(split, 1 - core, 2, keepdims=False)
    got = lax.ppermute(give, "tc", PAIR)
    pair = (keep.astype(jnp.float32) + got.astype(jnp.float32)).astype(value.dtype)
    return chip_reduce_scatter(jnp.transpose(pair, (1, 0, 2)))


def on_device(
    residual,
    context,
    attention_output_weight,
    adapter_down_maps,
    adapter_up_maps,
    adapter_storage_row,
    active_adapters,
    request_token_length,
    request_adapter_entry,
    expert_norm_gain,
    router_projection,
    expert_choice_pairs,
    expert_gate_weight,
    expert_up_weight,
    expert_down_weight,
):
    token_count = residual.shape[0]
    hidden_width = residual.shape[1]
    feature_share = context.shape[1]
    local_rows = adapter_down_maps.shape[0]
    adapter_rank_size = adapter_down_maps.shape[2]
    request_count = request_token_length.shape[1]
    share_width = hidden_width // (lax.axis_size("tz") * 2)
    share_start = (lax.axis_index("tz") * 2 + lax.axis_index("tc")) * share_width

    up_slice = lax.dynamic_slice_in_dim(adapter_up_maps, share_start, share_width, 2)
    packed = jnp.concatenate(
        [
            adapter_down_maps.reshape(local_rows, feature_share * adapter_rank_size),
            up_slice.reshape(local_rows, adapter_rank_size * share_width),
        ],
        axis=1,
    )
    req_count = lax.axis_size("ry") * lax.axis_size("rxz")
    all_packed = lax.all_to_all(
        jnp.broadcast_to(packed[None], (req_count,) + packed.shape),
        REQ,
        split_axis=0,
        concat_axis=0,
        tiled=True,
    ).reshape(req_count * local_rows, packed.shape[1])
    request_rows = adapter_storage_row[active_adapters[request_adapter_entry[0]]]
    picked = all_packed[request_rows]
    down_req = picked[:, : feature_share * adapter_rank_size].reshape(
        request_count, feature_share, adapter_rank_size
    )
    up_req = picked[:, feature_share * adapter_rank_size :].reshape(
        request_count * adapter_rank_size, share_width
    )
    down_joined = jnp.transpose(down_req, (1, 0, 2)).reshape(
        feature_share, request_count * adapter_rank_size
    )
    segment_hot = segment_onehot(request_token_length, token_count)
    low_all = jnp.dot(context, down_joined, preferred_element_type=jnp.float32)
    reduced_mask = jnp.repeat(segment_hot, adapter_rank_size, axis=1)
    low_part = jnp.where(reduced_mask, low_all, 0.0)
    low_total = tp_psum(low_part, lax.axis_size("tz") * 2).astype(jnp.bfloat16)
    lora_share = jnp.dot(low_total, up_req, preferred_element_type=jnp.float32)

    base = jnp.dot(context, attention_output_weight, preferred_element_type=jnp.float32)
    base_share = pair_reduce_scatter(base.astype(jnp.bfloat16), share_width)
    own_share = (base_share + lora_share).astype(jnp.bfloat16)
    head_sum = (
        jnp.transpose(tp_all_gather(own_share, lax.axis_size("tz") * 2), (1, 0, 2))
        .reshape(token_count, hidden_width)
        .astype(jnp.float32)
    )
    gain_all = expert_norm_gain.astype(jnp.float32)
    blended_rows = residual.astype(jnp.float32) + head_sum
    mean_square = jnp.mean(blended_rows * blended_rows, axis=1, keepdims=True)
    normed = (blended_rows * lax.rsqrt(mean_square + NORM_EPS) * gain_all).astype(jnp.bfloat16)
    mixed_share = lax.dynamic_slice_in_dim(blended_rows, share_start, share_width, 1)
    logits = jnp.dot(normed, router_projection, preferred_element_type=jnp.float32)
    expert_count = router_projection.shape[1]
    expert_range = jnp.arange(expert_count, dtype=jnp.int32)
    logit_first = jnp.sum(
        jnp.where(expert_choice_pairs[:, 0:1] == expert_range[None, :], logits, 0.0), axis=1
    )
    logit_second = jnp.sum(
        jnp.where(expert_choice_pairs[:, 1:2] == expert_range[None, :], logits, 0.0), axis=1
    )
    weight_first = 1.0 / (1.0 + jnp.exp(logit_second - logit_first))
    weight_second = 1.0 / (1.0 + jnp.exp(logit_first - logit_second))

    placement, first_hit, second_hit = route_tables(expert_choice_pairs, expert_count, CAP)
    send_rows = jnp.einsum(
        "est,td->esd", placement.astype(jnp.bfloat16), normed, preferred_element_type=jnp.float32
    ).astype(jnp.bfloat16)
    send_halves = send_rows.reshape(expert_count, CAP, 2, hidden_width // 2)
    core = lax.axis_index("tc")
    own_half = lax.dynamic_index_in_dim(send_halves, core, 2, keepdims=False)
    half_in = lax.all_to_all(own_half, "rxz", split_axis=0, concat_axis=0, tiled=True)
    other_in = lax.ppermute(half_in, "tc", PAIR)
    rows_in = jnp.where(
        core == 0,
        jnp.concatenate([half_in, other_in], axis=2),
        jnp.concatenate([other_in, half_in], axis=2),
    )
    rows_flat = rows_in.reshape(expert_count * CAP, hidden_width)
    gate_value = jnp.dot(rows_flat, expert_gate_weight[0], preferred_element_type=jnp.float32)
    up_value = jnp.dot(rows_flat, expert_up_weight[0], preferred_element_type=jnp.float32)
    hidden = (jax.nn.silu(gate_value) * up_value).astype(jnp.bfloat16)
    partial_value = jnp.dot(hidden, expert_down_weight[0], preferred_element_type=jnp.float32)
    chip_count = lax.axis_size("tz")
    partial_split = partial_value.astype(jnp.bfloat16).reshape(
        expert_count * CAP, chip_count, 2, share_width
    )
    keep_part = lax.dynamic_index_in_dim(partial_split, core, 2, keepdims=False)
    give_part = lax.dynamic_index_in_dim(partial_split, 1 - core, 2, keepdims=False)
    got_part = lax.ppermute(give_part, "tc", PAIR)
    pair_value = (keep_part.astype(jnp.float32) + got_part.astype(jnp.float32)).astype(jnp.bfloat16)
    chip_parts = lax.all_to_all(
        jnp.transpose(pair_value, (1, 0, 2)), "tz", split_axis=0, concat_axis=0, tiled=True
    )
    slot_value = jnp.sum(chip_parts.astype(jnp.float32), axis=0).astype(jnp.bfloat16)
    returned = lax.all_to_all(
        slot_value.reshape(expert_count, CAP, share_width),
        "rxz",
        split_axis=0,
        concat_axis=0,
        tiled=True,
    )
    token_weight = jnp.where(first_hit, weight_first[None, :], 0.0) + jnp.where(
        second_hit, weight_second[None, :], 0.0
    )
    scaled_place = placement.astype(jnp.float32) * token_weight[:, None, :]
    contribution = jnp.einsum(
        "est,esd->td",
        scaled_place,
        returned.astype(jnp.float32),
        precision=lax.Precision.HIGHEST,
        preferred_element_type=jnp.float32,
    )
    moe_share = contribution
    return (mixed_share + moe_share).astype(jnp.bfloat16)


def solution(mesh):
    req_size = mesh.shape["req"]
    plane = 8
    split_mesh = Mesh(
        mesh.devices.reshape(req_size // plane, plane, mesh.shape["tp"] // 2, 2),
        ("ry", "rxz", "tz", "tc"),
    )
    return jax.shard_map(
        on_device,
        mesh=split_mesh,
        in_specs=(
            P(REQ, None),
            P(REQ, TP),
            P(TP, None),
            P(REQ, TP, None),
            P(REQ, None, None),
            P(),
            P(),
            P(REQ, None),
            P(REQ, None),
            P(),
            P(),
            P(REQ, None),
            P(REQ, None, TP),
            P(REQ, None, TP),
            P(REQ, TP, None),
        ),
        out_specs=P(REQ, TP),
        check_vma=False,
    )
```

```python
import jax
import jax.numpy as jnp
from jax import lax
from jax.sharding import Mesh
from jax.sharding import PartitionSpec as P

CAP = 80


NORM_EPS = 1e-05

REQ = ("ry", "rxz")
TP = ("tz", "tc")
PAIR = [(0, 1), (1, 0)]


def segment_onehot(request_token_length, token_count):
    bounds = jnp.cumsum(request_token_length[0])
    position = jnp.arange(token_count, dtype=jnp.int32)
    segment = jnp.sum((position[:, None] >= bounds[None, :]).astype(jnp.int32), axis=1)
    slot_range = jnp.arange(request_token_length.shape[1], dtype=jnp.int32)
    return segment[:, None] == slot_range[None, :]


def route_tables(expert_choice_pairs, expert_count, capacity):
    expert_ids = jnp.arange(expert_count, dtype=jnp.int32)
    first_hit = expert_choice_pairs[None, :, 0] == expert_ids[:, None]
    second_hit = expert_choice_pairs[None, :, 1] == expert_ids[:, None]
    chosen = first_hit | second_hit
    slot_of = jnp.cumsum(chosen.astype(jnp.int32), axis=1) - 1
    slot_range = jnp.arange(capacity, dtype=jnp.int32)
    placement = chosen[:, None, :] & (slot_of[:, None, :] == slot_range[None, :, None])
    return (placement, first_hit, second_hit)


def shift_pairs(size, step):
    return [(source, (source + step) % size) for source in range(size)]


def chip_reduce_scatter(chunks):
    count = chunks.shape[0]
    place = lax.axis_index("tz")
    total = lax.dynamic_index_in_dim(chunks, place, 0, keepdims=False).astype(jnp.float32)
    for step in range(1, count):
        give = lax.dynamic_index_in_dim(chunks, (place + step) % count, 0, keepdims=False)
        total = total + lax.ppermute(give, "tz", shift_pairs(count, step)).astype(jnp.float32)
    return total


def tp_all_gather(piece, count):
    place = lax.axis_index("tz") * 2 + lax.axis_index("tc")
    got = [piece]
    for step in range(1, count):
        got.append(lax.ppermute(piece, TP, shift_pairs(count, step)))
    stacked = jnp.stack(got, axis=0)
    order = (place - jnp.arange(count, dtype=jnp.int32)) % count
    return jnp.take(stacked, order, axis=0)


def tp_psum(value, count):
    sent = value.astype(jnp.bfloat16)
    total = sent.astype(jnp.float32)
    for step in range(1, count):
        total = total + lax.ppermute(sent, TP, shift_pairs(count, step)).astype(jnp.float32)
    return total


def pair_reduce_scatter(value, share_width):
    rows = value.shape[0]
    chip_count = lax.axis_size("tz")
    core = lax.axis_index("tc")
    split = value.reshape(rows, chip_count, 2, share_width)
    keep = lax.dynamic_index_in_dim(split, core, 2, keepdims=False)
    give = lax.dynamic_index_in_dim(split, 1 - core, 2, keepdims=False)
    got = lax.ppermute(give, "tc", PAIR)
    pair = (keep.astype(jnp.float32) + got.astype(jnp.float32)).astype(value.dtype)
    return chip_reduce_scatter(jnp.transpose(pair, (1, 0, 2)))


def on_device(
    residual,
    context,
    attention_output_weight,
    adapter_down_maps,
    adapter_up_maps,
    adapter_storage_row,
    active_adapters,
    request_token_length,
    request_adapter_entry,
    expert_norm_gain,
    router_projection,
    expert_choice_pairs,
    expert_gate_weight,
    expert_up_weight,
    expert_down_weight,
):
    token_count = residual.shape[0]
    hidden_width = residual.shape[1]
    feature_share = context.shape[1]
    local_rows = adapter_down_maps.shape[0]
    adapter_rank_size = adapter_down_maps.shape[2]
    request_count = request_token_length.shape[1]
    share_width = hidden_width // (lax.axis_size("tz") * 2)
    share_start = (lax.axis_index("tz") * 2 + lax.axis_index("tc")) * share_width

    up_slice = lax.dynamic_slice_in_dim(adapter_up_maps, share_start, share_width, 2)
    packed = jnp.concatenate(
        [
            adapter_down_maps.reshape(local_rows, feature_share * adapter_rank_size),
            up_slice.reshape(local_rows, adapter_rank_size * share_width),
        ],
        axis=1,
    )
    req_count = lax.axis_size("ry") * lax.axis_size("rxz")
    all_packed = lax.all_to_all(
        jnp.broadcast_to(packed[None], (req_count,) + packed.shape),
        REQ,
        split_axis=0,
        concat_axis=0,
        tiled=True,
    ).reshape(req_count * local_rows, packed.shape[1])
    request_rows = adapter_storage_row[active_adapters[request_adapter_entry[0]]]
    picked = all_packed[request_rows]
    down_req = picked[:, : feature_share * adapter_rank_size].reshape(
        request_count, feature_share, adapter_rank_size
    )
    up_req = picked[:, feature_share * adapter_rank_size :].reshape(
        request_count * adapter_rank_size, share_width
    )
    down_joined = jnp.transpose(down_req, (1, 0, 2)).reshape(
        feature_share, request_count * adapter_rank_size
    )
    segment_hot = segment_onehot(request_token_length, token_count)
    low_all = jnp.dot(context, down_joined, preferred_element_type=jnp.float32)
    reduced_mask = jnp.repeat(segment_hot, adapter_rank_size, axis=1)
    low_part = jnp.where(reduced_mask, low_all, 0.0)
    low_total = tp_psum(low_part, lax.axis_size("tz") * 2).astype(jnp.bfloat16)
    lora_share = jnp.dot(low_total, up_req, preferred_element_type=jnp.float32)

    base = jnp.dot(context, attention_output_weight, preferred_element_type=jnp.float32)
    base_share = pair_reduce_scatter(base.astype(jnp.bfloat16), share_width)
    own_share = (base_share + lora_share).astype(jnp.bfloat16)
    head_sum = (
        jnp.transpose(tp_all_gather(own_share, lax.axis_size("tz") * 2), (1, 0, 2))
        .reshape(token_count, hidden_width)
        .astype(jnp.float32)
    )
    gain_all = expert_norm_gain.astype(jnp.float32)
    blended_rows = residual.astype(jnp.float32) + head_sum
    mean_square = jnp.mean(blended_rows * blended_rows, axis=1, keepdims=True)
    normed = (blended_rows * lax.rsqrt(mean_square + NORM_EPS) * gain_all).astype(jnp.bfloat16)
    mixed_share = lax.dynamic_slice_in_dim(blended_rows, share_start, share_width, 1)
    logits = jnp.dot(normed, router_projection, preferred_element_type=jnp.float32)
    expert_count = router_projection.shape[1]
    expert_range = jnp.arange(expert_count, dtype=jnp.int32)
    logit_first = jnp.sum(
        jnp.where(expert_choice_pairs[:, 0:1] == expert_range[None, :], logits, 0.0), axis=1
    )
    logit_second = jnp.sum(
        jnp.where(expert_choice_pairs[:, 1:2] == expert_range[None, :], logits, 0.0), axis=1
    )
    weight_first = 1.0 / (1.0 + jnp.exp(logit_second - logit_first))
    weight_second = 1.0 / (1.0 + jnp.exp(logit_first - logit_second))

    placement, first_hit, second_hit = route_tables(expert_choice_pairs, expert_count, CAP)
    send_rows = jnp.einsum(
        "est,td->esd", placement.astype(jnp.bfloat16), normed, preferred_element_type=jnp.float32
    ).astype(jnp.bfloat16)
    send_halves = send_rows.reshape(expert_count, CAP, 2, hidden_width // 2)
    core = lax.axis_index("tc")
    own_half = lax.dynamic_index_in_dim(send_halves, core, 2, keepdims=False)
    half_in = lax.all_to_all(own_half, "rxz", split_axis=0, concat_axis=0, tiled=True)
    other_in = lax.ppermute(half_in, "tc", PAIR)
    rows_in = jnp.where(
        core == 0,
        jnp.concatenate([half_in, other_in], axis=2),
        jnp.concatenate([other_in, half_in], axis=2),
    )
    rows_flat = rows_in.reshape(expert_count * CAP, hidden_width)
    gate_value = jnp.dot(rows_flat, expert_gate_weight[0], preferred_element_type=jnp.float32)
    up_value = jnp.dot(rows_flat, expert_up_weight[0], preferred_element_type=jnp.float32)
    hidden = (jax.nn.silu(gate_value) * up_value).astype(jnp.bfloat16)
    partial_value = jnp.dot(hidden, expert_down_weight[0], preferred_element_type=jnp.float32)
    chip_count = lax.axis_size("tz")
    partial_split = partial_value.astype(jnp.bfloat16).reshape(
        expert_count * CAP, chip_count, 2, share_width
    )
    keep_part = lax.dynamic_index_in_dim(partial_split, core, 2, keepdims=False)
    give_part = lax.dynamic_index_in_dim(partial_split, 1 - core, 2, keepdims=False)
    got_part = lax.ppermute(give_part, "tc", PAIR)
    pair_value = (keep_part.astype(jnp.float32) + got_part.astype(jnp.float32)).astype(jnp.bfloat16)
    slot_value = chip_reduce_scatter(jnp.transpose(pair_value, (1, 0, 2))).astype(jnp.bfloat16)
    returned = lax.all_to_all(
        slot_value.reshape(expert_count, CAP, share_width),
        "rxz",
        split_axis=0,
        concat_axis=0,
        tiled=True,
    )
    token_weight = jnp.where(first_hit, weight_first[None, :], 0.0) + jnp.where(
        second_hit, weight_second[None, :], 0.0
    )
    scaled_place = placement.astype(jnp.float32) * token_weight[:, None, :]
    contribution = jnp.einsum(
        "est,esd->td",
        scaled_place,
        returned.astype(jnp.float32),
        precision=lax.Precision.HIGHEST,
        preferred_element_type=jnp.float32,
    )
    moe_share = contribution
    return (mixed_share + moe_share).astype(jnp.bfloat16)


def solution(mesh):
    req_size = mesh.shape["req"]
    plane = 8
    split_mesh = Mesh(
        mesh.devices.reshape(req_size // plane, plane, mesh.shape["tp"] // 2, 2),
        ("ry", "rxz", "tz", "tc"),
    )
    return jax.shard_map(
        on_device,
        mesh=split_mesh,
        in_specs=(
            P(REQ, None),
            P(REQ, TP),
            P(TP, None),
            P(REQ, TP, None),
            P(REQ, None, None),
            P(),
            P(),
            P(REQ, None),
            P(REQ, None),
            P(),
            P(),
            P(REQ, None),
            P(REQ, None, TP),
            P(REQ, None, TP),
            P(REQ, TP, None),
        ),
        out_specs=P(REQ, TP),
        check_vma=False,
    )
```

```python
import jax
import jax.numpy as jnp
from jax import lax
from jax.sharding import Mesh
from jax.sharding import PartitionSpec as P

CAP = 80


NORM_EPS = 1e-05

REQ = ("ry", "rxz")
TP = ("tz", "tc")
PAIR = [(0, 1), (1, 0)]


def segment_onehot(request_token_length, token_count):
    bounds = jnp.cumsum(request_token_length[0])
    position = jnp.arange(token_count, dtype=jnp.int32)
    segment = jnp.sum((position[:, None] >= bounds[None, :]).astype(jnp.int32), axis=1)
    slot_range = jnp.arange(request_token_length.shape[1], dtype=jnp.int32)
    return segment[:, None] == slot_range[None, :]


def route_tables(expert_choice_pairs, expert_count, capacity):
    expert_ids = jnp.arange(expert_count, dtype=jnp.int32)
    first_hit = expert_choice_pairs[None, :, 0] == expert_ids[:, None]
    second_hit = expert_choice_pairs[None, :, 1] == expert_ids[:, None]
    chosen = first_hit | second_hit
    slot_of = jnp.cumsum(chosen.astype(jnp.int32), axis=1) - 1
    slot_range = jnp.arange(capacity, dtype=jnp.int32)
    placement = chosen[:, None, :] & (slot_of[:, None, :] == slot_range[None, :, None])
    return (placement, first_hit, second_hit)


def shift_pairs(size, step):
    return [(source, (source + step) % size) for source in range(size)]


def chip_reduce_scatter(chunks):
    count = chunks.shape[0]
    place = lax.axis_index("tz")
    total = lax.dynamic_index_in_dim(chunks, place, 0, keepdims=False).astype(jnp.float32)
    for step in range(1, count):
        give = lax.dynamic_index_in_dim(chunks, (place + step) % count, 0, keepdims=False)
        total = total + lax.ppermute(give, "tz", shift_pairs(count, step)).astype(jnp.float32)
    return total


def tp_all_gather(piece, count):
    place = lax.axis_index("tz") * 2 + lax.axis_index("tc")
    got = [piece]
    for step in range(1, count):
        got.append(lax.ppermute(piece, TP, shift_pairs(count, step)))
    stacked = jnp.stack(got, axis=0)
    order = (place - jnp.arange(count, dtype=jnp.int32)) % count
    return jnp.take(stacked, order, axis=0)


def tp_psum(value, count):
    sent = value.astype(jnp.bfloat16)
    total = sent.astype(jnp.float32)
    for step in range(1, count):
        total = total + lax.ppermute(sent, TP, shift_pairs(count, step)).astype(jnp.float32)
    return total


def pair_reduce_scatter(value, share_width):
    rows = value.shape[0]
    chip_count = lax.axis_size("tz")
    core = lax.axis_index("tc")
    split = value.reshape(rows, chip_count, 2, share_width)
    keep = lax.dynamic_index_in_dim(split, core, 2, keepdims=False)
    give = lax.dynamic_index_in_dim(split, 1 - core, 2, keepdims=False)
    got = lax.ppermute(give, "tc", PAIR)
    pair = (keep.astype(jnp.float32) + got.astype(jnp.float32)).astype(value.dtype)
    return chip_reduce_scatter(jnp.transpose(pair, (1, 0, 2)))


def on_device(
    residual,
    context,
    attention_output_weight,
    adapter_down_maps,
    adapter_up_maps,
    adapter_storage_row,
    active_adapters,
    request_token_length,
    request_adapter_entry,
    expert_norm_gain,
    router_projection,
    expert_choice_pairs,
    expert_gate_weight,
    expert_up_weight,
    expert_down_weight,
):
    token_count = residual.shape[0]
    hidden_width = residual.shape[1]
    feature_share = context.shape[1]
    local_rows = adapter_down_maps.shape[0]
    adapter_rank_size = adapter_down_maps.shape[2]
    request_count = request_token_length.shape[1]
    share_width = hidden_width // (lax.axis_size("tz") * 2)
    share_start = (lax.axis_index("tz") * 2 + lax.axis_index("tc")) * share_width

    up_slice = lax.dynamic_slice_in_dim(adapter_up_maps, share_start, share_width, 2)
    packed = jnp.concatenate(
        [
            adapter_down_maps.reshape(local_rows, feature_share * adapter_rank_size),
            up_slice.reshape(local_rows, adapter_rank_size * share_width),
        ],
        axis=1,
    )
    req_count = lax.axis_size("ry") * lax.axis_size("rxz")
    all_packed = lax.all_to_all(
        jnp.broadcast_to(packed[None], (req_count,) + packed.shape),
        REQ,
        split_axis=0,
        concat_axis=0,
        tiled=True,
    ).reshape(req_count * local_rows, packed.shape[1])
    request_rows = adapter_storage_row[active_adapters[request_adapter_entry[0]]]
    picked = all_packed[request_rows]
    down_req = picked[:, : feature_share * adapter_rank_size].reshape(
        request_count, feature_share, adapter_rank_size
    )
    up_req = picked[:, feature_share * adapter_rank_size :].reshape(
        request_count * adapter_rank_size, share_width
    )
    down_joined = jnp.transpose(down_req, (1, 0, 2)).reshape(
        feature_share, request_count * adapter_rank_size
    )
    segment_hot = segment_onehot(request_token_length, token_count)
    low_all = jnp.dot(context, down_joined, preferred_element_type=jnp.float32)
    reduced_mask = jnp.repeat(segment_hot, adapter_rank_size, axis=1)
    low_part = jnp.where(reduced_mask, low_all, 0.0)
    low_total = tp_psum(low_part, lax.axis_size("tz") * 2).astype(jnp.bfloat16)
    lora_share = jnp.dot(low_total, up_req, preferred_element_type=jnp.float32)

    base = jnp.dot(context, attention_output_weight, preferred_element_type=jnp.float32)
    base_share = pair_reduce_scatter(base.astype(jnp.bfloat16), share_width)
    own_share = (base_share + lora_share).astype(jnp.bfloat16)
    head_sum = (
        jnp.transpose(tp_all_gather(own_share, lax.axis_size("tz") * 2), (1, 0, 2))
        .reshape(token_count, hidden_width)
        .astype(jnp.float32)
    )
    gain_all = expert_norm_gain.astype(jnp.float32)
    blended_rows = residual.astype(jnp.float32) + head_sum
    mean_square = jnp.mean(blended_rows * blended_rows, axis=1, keepdims=True)
    normed = (blended_rows * lax.rsqrt(mean_square + NORM_EPS) * gain_all).astype(jnp.bfloat16)
    mixed_share = lax.dynamic_slice_in_dim(blended_rows, share_start, share_width, 1)
    logits = jnp.dot(normed, router_projection, preferred_element_type=jnp.float32)
    expert_count = router_projection.shape[1]
    expert_range = jnp.arange(expert_count, dtype=jnp.int32)
    logit_first = jnp.sum(
        jnp.where(expert_choice_pairs[:, 0:1] == expert_range[None, :], logits, 0.0), axis=1
    )
    logit_second = jnp.sum(
        jnp.where(expert_choice_pairs[:, 1:2] == expert_range[None, :], logits, 0.0), axis=1
    )
    weight_first = 1.0 / (1.0 + jnp.exp(logit_second - logit_first))
    weight_second = 1.0 / (1.0 + jnp.exp(logit_first - logit_second))

    placement, first_hit, second_hit = route_tables(expert_choice_pairs, expert_count, CAP)
    send_rows = jnp.einsum(
        "est,td->esd", placement.astype(jnp.bfloat16), normed, preferred_element_type=jnp.float32
    ).astype(jnp.bfloat16)
    send_halves = send_rows.reshape(expert_count, CAP, 2, hidden_width // 2)
    core = lax.axis_index("tc")
    own_half = lax.dynamic_index_in_dim(send_halves, core, 2, keepdims=False)
    half_in = lax.all_to_all(own_half, "rxz", split_axis=0, concat_axis=0, tiled=True)
    other_in = lax.ppermute(half_in, "tc", PAIR)
    rows_in = jnp.where(
        core == 0,
        jnp.concatenate([half_in, other_in], axis=2),
        jnp.concatenate([other_in, half_in], axis=2),
    )
    chip_count = lax.axis_size("tz")
    piece_count = 2
    piece_rows = expert_count * CAP // piece_count
    rows_flat = rows_in.reshape(piece_count, piece_rows, hidden_width)
    slot_pieces = []
    for piece in range(piece_count):
        rows_piece = rows_flat[piece]
        gate_value = jnp.dot(rows_piece, expert_gate_weight[0], preferred_element_type=jnp.float32)
        up_value = jnp.dot(rows_piece, expert_up_weight[0], preferred_element_type=jnp.float32)
        hidden = (jax.nn.silu(gate_value) * up_value).astype(jnp.bfloat16)
        partial_value = jnp.dot(hidden, expert_down_weight[0], preferred_element_type=jnp.float32)
        partial_split = partial_value.astype(jnp.bfloat16).reshape(
            piece_rows, chip_count, 2, share_width
        )
        keep_part = lax.dynamic_index_in_dim(partial_split, core, 2, keepdims=False)
        give_part = lax.dynamic_index_in_dim(partial_split, 1 - core, 2, keepdims=False)
        got_part = lax.ppermute(give_part, "tc", PAIR)
        pair_value = (keep_part.astype(jnp.float32) + got_part.astype(jnp.float32)).astype(
            jnp.bfloat16
        )
        slot_pieces.append(
            chip_reduce_scatter(jnp.transpose(pair_value, (1, 0, 2))).astype(jnp.bfloat16)
        )
    slot_value = jnp.concatenate(slot_pieces, axis=0)
    returned = lax.all_to_all(
        slot_value.reshape(expert_count, CAP, share_width),
        "rxz",
        split_axis=0,
        concat_axis=0,
        tiled=True,
    )
    token_weight = jnp.where(first_hit, weight_first[None, :], 0.0) + jnp.where(
        second_hit, weight_second[None, :], 0.0
    )
    scaled_place = placement.astype(jnp.float32) * token_weight[:, None, :]
    contribution = jnp.einsum(
        "est,esd->td",
        scaled_place,
        returned.astype(jnp.float32),
        precision=lax.Precision.HIGHEST,
        preferred_element_type=jnp.float32,
    )
    moe_share = contribution
    return (mixed_share + moe_share).astype(jnp.bfloat16)


def solution(mesh):
    req_size = mesh.shape["req"]
    plane = 8
    split_mesh = Mesh(
        mesh.devices.reshape(req_size // plane, plane, mesh.shape["tp"] // 2, 2),
        ("ry", "rxz", "tz", "tc"),
    )
    return jax.shard_map(
        on_device,
        mesh=split_mesh,
        in_specs=(
            P(REQ, None),
            P(REQ, TP),
            P(TP, None),
            P(REQ, TP, None),
            P(REQ, None, None),
            P(),
            P(),
            P(REQ, None),
            P(REQ, None),
            P(),
            P(),
            P(REQ, None),
            P(REQ, None, TP),
            P(REQ, None, TP),
            P(REQ, TP, None),
        ),
        out_specs=P(REQ, TP),
        check_vma=False,
    )
```

```python
import jax
import jax.numpy as jnp
from jax import lax
from jax.sharding import Mesh
from jax.sharding import PartitionSpec as P

CAP = 80


NORM_EPS = 1e-05

REQ = ("ry", "rxz")
TP = ("tz", "tc")
PAIR = [(0, 1), (1, 0)]


def segment_onehot(request_token_length, token_count):
    bounds = jnp.cumsum(request_token_length[0])
    position = jnp.arange(token_count, dtype=jnp.int32)
    segment = jnp.sum((position[:, None] >= bounds[None, :]).astype(jnp.int32), axis=1)
    slot_range = jnp.arange(request_token_length.shape[1], dtype=jnp.int32)
    return segment[:, None] == slot_range[None, :]


def route_tables(expert_choice_pairs, expert_count, capacity):
    expert_ids = jnp.arange(expert_count, dtype=jnp.int32)
    first_hit = expert_choice_pairs[None, :, 0] == expert_ids[:, None]
    second_hit = expert_choice_pairs[None, :, 1] == expert_ids[:, None]
    chosen = first_hit | second_hit
    slot_of = jnp.cumsum(chosen.astype(jnp.int32), axis=1) - 1
    slot_range = jnp.arange(capacity, dtype=jnp.int32)
    placement = chosen[:, None, :] & (slot_of[:, None, :] == slot_range[None, :, None])
    return (placement, first_hit, second_hit)


def shift_pairs(size, step):
    return [(source, (source + step) % size) for source in range(size)]


def chip_reduce_scatter(chunks):
    count = chunks.shape[0]
    place = lax.axis_index("tz")
    total = lax.dynamic_index_in_dim(chunks, place, 0, keepdims=False).astype(jnp.float32)
    for step in range(1, count):
        give = lax.dynamic_index_in_dim(chunks, (place + step) % count, 0, keepdims=False)
        total = total + lax.ppermute(give, "tz", shift_pairs(count, step)).astype(jnp.float32)
    return total


def tp_all_gather(piece, count):
    place = lax.axis_index("tz") * 2 + lax.axis_index("tc")
    got = [piece]
    for step in range(1, count):
        got.append(lax.ppermute(piece, TP, shift_pairs(count, step)))
    stacked = jnp.stack(got, axis=0)
    order = (place - jnp.arange(count, dtype=jnp.int32)) % count
    return jnp.take(stacked, order, axis=0)


def tp_psum(value, count):
    sent = value.astype(jnp.bfloat16)
    total = sent.astype(jnp.float32)
    for step in range(1, count):
        total = total + lax.ppermute(sent, TP, shift_pairs(count, step)).astype(jnp.float32)
    return total


def pair_reduce_scatter(value, share_width):
    rows = value.shape[0]
    chip_count = lax.axis_size("tz")
    core = lax.axis_index("tc")
    split = value.reshape(rows, chip_count, 2, share_width)
    keep = lax.dynamic_index_in_dim(split, core, 2, keepdims=False)
    give = lax.dynamic_index_in_dim(split, 1 - core, 2, keepdims=False)
    got = lax.ppermute(give, "tc", PAIR)
    pair = (keep.astype(jnp.float32) + got.astype(jnp.float32)).astype(value.dtype)
    return chip_reduce_scatter(jnp.transpose(pair, (1, 0, 2)))


def on_device(
    residual,
    context,
    attention_output_weight,
    adapter_down_maps,
    adapter_up_maps,
    adapter_storage_row,
    active_adapters,
    request_token_length,
    request_adapter_entry,
    expert_norm_gain,
    router_projection,
    expert_choice_pairs,
    expert_gate_weight,
    expert_up_weight,
    expert_down_weight,
):
    token_count = residual.shape[0]
    hidden_width = residual.shape[1]
    feature_share = context.shape[1]
    local_rows = adapter_down_maps.shape[0]
    adapter_rank_size = adapter_down_maps.shape[2]
    request_count = request_token_length.shape[1]
    share_width = hidden_width // (lax.axis_size("tz") * 2)
    share_start = (lax.axis_index("tz") * 2 + lax.axis_index("tc")) * share_width

    up_slice = lax.dynamic_slice_in_dim(adapter_up_maps, share_start, share_width, 2)
    packed = jnp.concatenate(
        [
            adapter_down_maps.reshape(local_rows, feature_share * adapter_rank_size),
            up_slice.reshape(local_rows, adapter_rank_size * share_width),
        ],
        axis=1,
    )
    req_count = lax.axis_size("ry") * lax.axis_size("rxz")
    all_packed = lax.all_to_all(
        jnp.broadcast_to(packed[None], (req_count,) + packed.shape),
        REQ,
        split_axis=0,
        concat_axis=0,
        tiled=True,
    ).reshape(req_count * local_rows, packed.shape[1])
    request_rows = adapter_storage_row[active_adapters[request_adapter_entry[0]]]
    picked = all_packed[request_rows]
    down_req = picked[:, : feature_share * adapter_rank_size].reshape(
        request_count, feature_share, adapter_rank_size
    )
    up_req = picked[:, feature_share * adapter_rank_size :].reshape(
        request_count * adapter_rank_size, share_width
    )
    down_joined = jnp.transpose(down_req, (1, 0, 2)).reshape(
        feature_share, request_count * adapter_rank_size
    )
    segment_hot = segment_onehot(request_token_length, token_count)
    low_all = jnp.dot(context, down_joined, preferred_element_type=jnp.float32)
    reduced_mask = jnp.repeat(segment_hot, adapter_rank_size, axis=1)
    low_own = jnp.sum(
        jnp.where(
            segment_hot[:, :, None],
            low_all.reshape(token_count, request_count, adapter_rank_size),
            0.0,
        ),
        axis=1,
    )
    low_sum = tp_psum(low_own, lax.axis_size("tz") * 2).astype(jnp.bfloat16)
    low_total = jnp.where(
        reduced_mask, jnp.tile(low_sum, (1, request_count)), jnp.zeros((), jnp.bfloat16)
    )
    lora_share = jnp.dot(low_total, up_req, preferred_element_type=jnp.float32)

    base = jnp.dot(context, attention_output_weight, preferred_element_type=jnp.float32)
    base_share = pair_reduce_scatter(base.astype(jnp.bfloat16), share_width)
    own_share = (base_share + lora_share).astype(jnp.bfloat16)
    head_sum = (
        jnp.transpose(tp_all_gather(own_share, lax.axis_size("tz") * 2), (1, 0, 2))
        .reshape(token_count, hidden_width)
        .astype(jnp.float32)
    )
    gain_all = expert_norm_gain.astype(jnp.float32)
    blended_rows = residual.astype(jnp.float32) + head_sum
    mean_square = jnp.mean(blended_rows * blended_rows, axis=1, keepdims=True)
    normed = (blended_rows * lax.rsqrt(mean_square + NORM_EPS) * gain_all).astype(jnp.bfloat16)
    mixed_share = lax.dynamic_slice_in_dim(blended_rows, share_start, share_width, 1)
    logits = jnp.dot(normed, router_projection, preferred_element_type=jnp.float32)
    expert_count = router_projection.shape[1]
    expert_range = jnp.arange(expert_count, dtype=jnp.int32)
    logit_first = jnp.sum(
        jnp.where(expert_choice_pairs[:, 0:1] == expert_range[None, :], logits, 0.0), axis=1
    )
    logit_second = jnp.sum(
        jnp.where(expert_choice_pairs[:, 1:2] == expert_range[None, :], logits, 0.0), axis=1
    )
    weight_first = 1.0 / (1.0 + jnp.exp(logit_second - logit_first))
    weight_second = 1.0 / (1.0 + jnp.exp(logit_first - logit_second))

    placement, first_hit, second_hit = route_tables(expert_choice_pairs, expert_count, CAP)
    send_rows = jnp.einsum(
        "est,td->esd", placement.astype(jnp.bfloat16), normed, preferred_element_type=jnp.float32
    ).astype(jnp.bfloat16)
    send_halves = send_rows.reshape(expert_count, CAP, 2, hidden_width // 2)
    core = lax.axis_index("tc")
    own_half = lax.dynamic_index_in_dim(send_halves, core, 2, keepdims=False)
    half_in = lax.all_to_all(own_half, "rxz", split_axis=0, concat_axis=0, tiled=True)
    other_in = lax.ppermute(half_in, "tc", PAIR)
    rows_in = jnp.where(
        core == 0,
        jnp.concatenate([half_in, other_in], axis=2),
        jnp.concatenate([other_in, half_in], axis=2),
    )
    rows_flat = rows_in.reshape(expert_count * CAP, hidden_width)
    gate_value = jnp.dot(rows_flat, expert_gate_weight[0], preferred_element_type=jnp.float32)
    up_value = jnp.dot(rows_flat, expert_up_weight[0], preferred_element_type=jnp.float32)
    hidden = (jax.nn.silu(gate_value) * up_value).astype(jnp.bfloat16)
    partial_value = jnp.dot(hidden, expert_down_weight[0], preferred_element_type=jnp.float32)
    chip_count = lax.axis_size("tz")
    partial_split = partial_value.astype(jnp.bfloat16).reshape(
        expert_count * CAP, chip_count, 2, share_width
    )
    keep_part = lax.dynamic_index_in_dim(partial_split, core, 2, keepdims=False)
    give_part = lax.dynamic_index_in_dim(partial_split, 1 - core, 2, keepdims=False)
    got_part = lax.ppermute(give_part, "tc", PAIR)
    pair_value = (keep_part.astype(jnp.float32) + got_part.astype(jnp.float32)).astype(jnp.bfloat16)
    slot_value = chip_reduce_scatter(jnp.transpose(pair_value, (1, 0, 2))).astype(jnp.bfloat16)
    returned = lax.all_to_all(
        slot_value.reshape(expert_count, CAP, share_width),
        "rxz",
        split_axis=0,
        concat_axis=0,
        tiled=True,
    )
    token_weight = jnp.where(first_hit, weight_first[None, :], 0.0) + jnp.where(
        second_hit, weight_second[None, :], 0.0
    )
    scaled_place = placement.astype(jnp.float32) * token_weight[:, None, :]
    contribution = jnp.einsum(
        "est,esd->td",
        scaled_place,
        returned.astype(jnp.float32),
        precision=lax.Precision.HIGHEST,
        preferred_element_type=jnp.float32,
    )
    moe_share = contribution
    return (mixed_share + moe_share).astype(jnp.bfloat16)


def solution(mesh):
    req_size = mesh.shape["req"]
    plane = 8
    split_mesh = Mesh(
        mesh.devices.reshape(req_size // plane, plane, mesh.shape["tp"] // 2, 2),
        ("ry", "rxz", "tz", "tc"),
    )
    return jax.shard_map(
        on_device,
        mesh=split_mesh,
        in_specs=(
            P(REQ, None),
            P(REQ, TP),
            P(TP, None),
            P(REQ, TP, None),
            P(REQ, None, None),
            P(),
            P(),
            P(REQ, None),
            P(REQ, None),
            P(),
            P(),
            P(REQ, None),
            P(REQ, None, TP),
            P(REQ, None, TP),
            P(REQ, TP, None),
        ),
        out_specs=P(REQ, TP),
        check_vma=False,
    )
```

```python
import jax
import jax.numpy as jnp
from jax import lax
from jax.sharding import Mesh
from jax.sharding import PartitionSpec as P

CAP = 80


NORM_EPS = 1e-05

REQ = ("ry", "rxz")
TP = ("tz", "tc")
PAIR = [(0, 1), (1, 0)]


def segment_onehot(request_token_length, token_count):
    bounds = jnp.cumsum(request_token_length[0])
    position = jnp.arange(token_count, dtype=jnp.int32)
    segment = jnp.sum((position[:, None] >= bounds[None, :]).astype(jnp.int32), axis=1)
    slot_range = jnp.arange(request_token_length.shape[1], dtype=jnp.int32)
    return segment[:, None] == slot_range[None, :]


def route_tables(expert_choice_pairs, expert_count, capacity):
    expert_ids = jnp.arange(expert_count, dtype=jnp.int32)
    first_hit = expert_choice_pairs[None, :, 0] == expert_ids[:, None]
    second_hit = expert_choice_pairs[None, :, 1] == expert_ids[:, None]
    chosen = first_hit | second_hit
    slot_of = jnp.cumsum(chosen.astype(jnp.int32), axis=1) - 1
    slot_range = jnp.arange(capacity, dtype=jnp.int32)
    placement = chosen[:, None, :] & (slot_of[:, None, :] == slot_range[None, :, None])
    return (placement, first_hit, second_hit)


def shift_pairs(size, step):
    return [(source, (source + step) % size) for source in range(size)]


def chip_reduce_scatter(chunks):
    count = chunks.shape[0]
    place = lax.axis_index("tz")
    total = lax.dynamic_index_in_dim(chunks, place, 0, keepdims=False).astype(jnp.float32)
    for step in range(1, count):
        give = lax.dynamic_index_in_dim(chunks, (place + step) % count, 0, keepdims=False)
        total = total + lax.ppermute(give, "tz", shift_pairs(count, step)).astype(jnp.float32)
    return total


def tp_all_gather(piece, count):
    place = lax.axis_index("tz") * 2 + lax.axis_index("tc")
    got = [piece]
    for step in range(1, count):
        got.append(lax.ppermute(piece, TP, shift_pairs(count, step)))
    stacked = jnp.stack(got, axis=0)
    order = (place - jnp.arange(count, dtype=jnp.int32)) % count
    return jnp.take(stacked, order, axis=0)


def chip_pair_gather(piece):
    count = lax.axis_size("tz")
    place = lax.axis_index("tz")
    core = lax.axis_index("tc")
    got = [piece]
    for step in range(1, count):
        got.append(lax.ppermute(piece, "tz", shift_pairs(count, step)))
    order = (place - jnp.arange(count, dtype=jnp.int32)) % count
    chips = jnp.take(jnp.stack(got, axis=1), order, axis=1)
    other = lax.ppermute(chips, "tc", PAIR)
    return jnp.where(
        core == 0, jnp.stack([chips, other], axis=2), jnp.stack([other, chips], axis=2)
    )


def tp_psum(value, count):
    sent = value.astype(jnp.bfloat16)
    total = sent.astype(jnp.float32)
    for step in range(1, count):
        total = total + lax.ppermute(sent, TP, shift_pairs(count, step)).astype(jnp.float32)
    return total


def pair_reduce_scatter(value, share_width):
    rows = value.shape[0]
    chip_count = lax.axis_size("tz")
    core = lax.axis_index("tc")
    split = value.reshape(rows, chip_count, 2, share_width)
    keep = lax.dynamic_index_in_dim(split, core, 2, keepdims=False)
    give = lax.dynamic_index_in_dim(split, 1 - core, 2, keepdims=False)
    got = lax.ppermute(give, "tc", PAIR)
    pair = (keep.astype(jnp.float32) + got.astype(jnp.float32)).astype(value.dtype)
    return chip_reduce_scatter(jnp.transpose(pair, (1, 0, 2)))


def on_device(
    residual,
    context,
    attention_output_weight,
    adapter_down_maps,
    adapter_up_maps,
    adapter_storage_row,
    active_adapters,
    request_token_length,
    request_adapter_entry,
    expert_norm_gain,
    router_projection,
    expert_choice_pairs,
    expert_gate_weight,
    expert_up_weight,
    expert_down_weight,
):
    token_count = residual.shape[0]
    hidden_width = residual.shape[1]
    feature_share = context.shape[1]
    local_rows = adapter_down_maps.shape[0]
    adapter_rank_size = adapter_down_maps.shape[2]
    request_count = request_token_length.shape[1]
    share_width = hidden_width // (lax.axis_size("tz") * 2)
    share_start = (lax.axis_index("tz") * 2 + lax.axis_index("tc")) * share_width

    up_slice = lax.dynamic_slice_in_dim(adapter_up_maps, share_start, share_width, 2)
    packed = jnp.concatenate(
        [
            adapter_down_maps.reshape(local_rows, feature_share * adapter_rank_size),
            up_slice.reshape(local_rows, adapter_rank_size * share_width),
        ],
        axis=1,
    )
    req_count = lax.axis_size("ry") * lax.axis_size("rxz")
    all_packed = lax.all_to_all(
        jnp.broadcast_to(packed[None], (req_count,) + packed.shape),
        REQ,
        split_axis=0,
        concat_axis=0,
        tiled=True,
    ).reshape(req_count * local_rows, packed.shape[1])
    request_rows = adapter_storage_row[active_adapters[request_adapter_entry[0]]]
    picked = all_packed[request_rows]
    down_req = picked[:, : feature_share * adapter_rank_size].reshape(
        request_count, feature_share, adapter_rank_size
    )
    up_req = picked[:, feature_share * adapter_rank_size :].reshape(
        request_count * adapter_rank_size, share_width
    )
    down_joined = jnp.transpose(down_req, (1, 0, 2)).reshape(
        feature_share, request_count * adapter_rank_size
    )
    segment_hot = segment_onehot(request_token_length, token_count)
    low_all = jnp.dot(context, down_joined, preferred_element_type=jnp.float32)
    reduced_mask = jnp.repeat(segment_hot, adapter_rank_size, axis=1)
    low_part = jnp.where(reduced_mask, low_all, 0.0)
    low_total = tp_psum(low_part, lax.axis_size("tz") * 2).astype(jnp.bfloat16)
    lora_share = jnp.dot(low_total, up_req, preferred_element_type=jnp.float32)

    base = jnp.dot(context, attention_output_weight, preferred_element_type=jnp.float32)
    base_share = pair_reduce_scatter(base.astype(jnp.bfloat16), share_width)
    own_share = (base_share + lora_share).astype(jnp.bfloat16)
    head_sum = chip_pair_gather(own_share).reshape(token_count, hidden_width).astype(jnp.float32)
    gain_all = expert_norm_gain.astype(jnp.float32)
    blended_rows = residual.astype(jnp.float32) + head_sum
    mean_square = jnp.mean(blended_rows * blended_rows, axis=1, keepdims=True)
    normed = (blended_rows * lax.rsqrt(mean_square + NORM_EPS) * gain_all).astype(jnp.bfloat16)
    mixed_share = lax.dynamic_slice_in_dim(blended_rows, share_start, share_width, 1)
    logits = jnp.dot(normed, router_projection, preferred_element_type=jnp.float32)
    expert_count = router_projection.shape[1]
    expert_range = jnp.arange(expert_count, dtype=jnp.int32)
    logit_first = jnp.sum(
        jnp.where(expert_choice_pairs[:, 0:1] == expert_range[None, :], logits, 0.0), axis=1
    )
    logit_second = jnp.sum(
        jnp.where(expert_choice_pairs[:, 1:2] == expert_range[None, :], logits, 0.0), axis=1
    )
    weight_first = 1.0 / (1.0 + jnp.exp(logit_second - logit_first))
    weight_second = 1.0 / (1.0 + jnp.exp(logit_first - logit_second))

    placement, first_hit, second_hit = route_tables(expert_choice_pairs, expert_count, CAP)
    send_rows = jnp.einsum(
        "est,td->esd", placement.astype(jnp.bfloat16), normed, preferred_element_type=jnp.float32
    ).astype(jnp.bfloat16)
    send_halves = send_rows.reshape(expert_count, CAP, 2, hidden_width // 2)
    core = lax.axis_index("tc")
    own_half = lax.dynamic_index_in_dim(send_halves, core, 2, keepdims=False)
    half_in = lax.all_to_all(own_half, "rxz", split_axis=0, concat_axis=0, tiled=True)
    other_in = lax.ppermute(half_in, "tc", PAIR)
    rows_in = jnp.where(
        core == 0,
        jnp.concatenate([half_in, other_in], axis=2),
        jnp.concatenate([other_in, half_in], axis=2),
    )
    rows_flat = rows_in.reshape(expert_count * CAP, hidden_width)
    gate_value = jnp.dot(rows_flat, expert_gate_weight[0], preferred_element_type=jnp.float32)
    up_value = jnp.dot(rows_flat, expert_up_weight[0], preferred_element_type=jnp.float32)
    hidden = (jax.nn.silu(gate_value) * up_value).astype(jnp.bfloat16)
    partial_value = jnp.dot(hidden, expert_down_weight[0], preferred_element_type=jnp.float32)
    chip_count = lax.axis_size("tz")
    partial_split = partial_value.astype(jnp.bfloat16).reshape(
        expert_count * CAP, chip_count, 2, share_width
    )
    keep_part = lax.dynamic_index_in_dim(partial_split, core, 2, keepdims=False)
    give_part = lax.dynamic_index_in_dim(partial_split, 1 - core, 2, keepdims=False)
    got_part = lax.ppermute(give_part, "tc", PAIR)
    pair_value = (keep_part.astype(jnp.float32) + got_part.astype(jnp.float32)).astype(jnp.bfloat16)
    slot_value = chip_reduce_scatter(jnp.transpose(pair_value, (1, 0, 2))).astype(jnp.bfloat16)
    returned = lax.all_to_all(
        slot_value.reshape(expert_count, CAP, share_width),
        "rxz",
        split_axis=0,
        concat_axis=0,
        tiled=True,
    )
    token_weight = jnp.where(first_hit, weight_first[None, :], 0.0) + jnp.where(
        second_hit, weight_second[None, :], 0.0
    )
    scaled_place = placement.astype(jnp.float32) * token_weight[:, None, :]
    contribution = jnp.einsum(
        "est,esd->td",
        scaled_place,
        returned.astype(jnp.float32),
        precision=lax.Precision.HIGHEST,
        preferred_element_type=jnp.float32,
    )
    moe_share = contribution
    return (mixed_share + moe_share).astype(jnp.bfloat16)


def solution(mesh):
    req_size = mesh.shape["req"]
    plane = 8
    split_mesh = Mesh(
        mesh.devices.reshape(req_size // plane, plane, mesh.shape["tp"] // 2, 2),
        ("ry", "rxz", "tz", "tc"),
    )
    return jax.shard_map(
        on_device,
        mesh=split_mesh,
        in_specs=(
            P(REQ, None),
            P(REQ, TP),
            P(TP, None),
            P(REQ, TP, None),
            P(REQ, None, None),
            P(),
            P(),
            P(REQ, None),
            P(REQ, None),
            P(),
            P(),
            P(REQ, None),
            P(REQ, None, TP),
            P(REQ, None, TP),
            P(REQ, TP, None),
        ),
        out_specs=P(REQ, TP),
        check_vma=False,
    )
```
